512 devices in a mesh: sat: 16 (over z, core), seg: 32 (over y, x).
Axes of the slice: x: 4, y: 8, z: 8, core: 2. Of those that a mesh axis runs over, the one named last changes fastest.
Arguments:
- sens_params: bfloat16 [16, 32, 320, 1024], P('sat', 'seg'), may hold values from -0.59765625 to 0.59765625
- sens_state: bfloat16 [16, 32, 320, 64], P('sat', 'seg'), may hold values from -0.59765625 to 0.59765625
- misfit: float32 [16, 32, 320], P('sat', 'seg'), may hold values from -6 to 6
- depth: float32 [16, 32, 320], P('sat', 'seg'), may hold values from 0.2 to 0.9
- cycle_count: int32 [16, 32], P('sat', 'seg'), may hold values from 80 to 320, as said below
- node_side: int32 [16, 32, 320], P('sat', 'seg'), may hold values from 0 to 1, as said below
- transition: bfloat16 [16, 32, 64, 64], P('sat', 'seg'), may hold values from -0.75 to 0.75
- cont_sens: bfloat16 [16, 32, 64, 1024], P('sat', 'seg'), may hold values from -0.59765625 to 0.59765625
- noise_root: float32 [16, 32, 64, 64], P('sat', 'seg'), may hold values from -0.4 to 0.4
- cont_misfit: float32 [16, 32, 64], P('sat', 'seg'), may hold values from -6 to 6
Outputs:
- gram_params: float32 [1024, 1024], P('sat')
- grad_params: float32 [1024], replicated
- node_hess: float32 [16, 32, 64, 64], P('sat', 'seg')
- node_cross: float32 [16, 32, 64, 1024], P('sat', 'seg')
- node_grad: float32 [16, 32, 64], P('sat', 'seg')
- node_coupling: float32 [16, 32, 64, 64], P('sat', 'seg')
The draws below stay inside these ranges and needn't reach their ends.
Inputs may be any that keep to these rules, and one draw needn't show every extreme that they name: `cycle_count`: in every segment some satellite has exactly 320 cycles. `node_side`: along the cycles of one satellite's segment the value never falls, and both values occur.
All inputs are finite; a program needn't handle non-finite values.
Results may differ from the reference program's by a relative error of at most 0.0015.
The reference program's roundings to bfloat16 on the way (of `weighted_sens`, `weighted_res`, `state_pair`, `param_map` and `cont_res`) count: a program that leaves them out, or rounds other values in their place, can miss the bound.
Values sent between devices are 32-bit elements; how exact they have to be, the bound alone decides.
A program may use at most 64 MiB of HBM per device.

```python
import jax
import jax.numpy as jnp
from jax import lax

P_SIZE = 1024
S = 64
M = 320
SATS = 16
SEGS = 32


def draw_cycle_count(key, part):
    base = jax.random.randint(jax.random.fold_in(key, 11), (SATS, SEGS), M // 4, M + 1)
    chosen = jax.random.randint(jax.random.fold_in(key, 12), (SEGS,), 0, SATS)
    full_rows = jnp.arange(SATS)[:, None] == chosen[None, :]
    return jnp.where(full_rows, M, base).astype(jnp.int32)


def draw_node_side(key, part):
    cut_point = jax.random.randint(jax.random.fold_in(key, 13), (SATS, SEGS, 1), 1, M)
    return (jnp.arange(M)[None, None, :] >= cut_point).astype(jnp.int32)


def raised(values, rng, source, target, shards_of, factor):
    def block_of(position):
        return (jnp.arange(values.shape[position]) // (values.shape[position] // shards_of)).reshape((-1,) + (1,) * (values.ndim - 1 - position))

    first = jax.random.permutation(rng, shards_of)[block_of(target)]
    other_side = (block_of(target) + shards_of // 2) % shards_of
    return jnp.where((block_of(source) == first) | (block_of(source) == other_side), factor * values, values)


def level_of(own_key, shape, shards, least, largest):
    def one(position, parts):
        heights = jax.random.uniform(jax.random.fold_in(jax.random.fold_in(own_key, 6), position), (parts,), jnp.float32, least / len(shards), largest / len(shards))
        return jnp.repeat(jnp.exp(heights), shape[position] // parts).reshape((-1,) + (1,) * (len(shape) - position - 1))

    loudness = one(*shards[0])
    for cut in shards[1:]:
        loudness = loudness * one(*cut)
    return loudness


def gaussian(rng, dims, width, reach, shards=(), kind=jnp.bfloat16):
    entries = jax.random.normal(rng, dims, jnp.float32) * width
    if len(shards) > 0:
        entries = level_of(rng, dims, shards, -0.22, 0.18) * entries
    return jnp.clip(entries, min=-reach, max=reach).astype(kind)


def bell_draw_with(key, extent, deviation, limit, split, heavy, kind=jnp.bfloat16):
    values = deviation * jax.random.normal(key, extent, jnp.float32)
    if split:
        values = values * level_of(key, extent, split, -0.22, 0.18)
    return jnp.clip(raised(values, jax.random.fold_in(key, 3), *heavy), -limit, limit).astype(kind)


def setup_inputs(seed: int = 0) -> dict:
    seeds = jax.random.split(jax.random.key(seed), 11)
    sens_params = bell_draw_with(seeds[0], (SATS, SEGS, M, P_SIZE), 0.1, 0.59765625, ((0, 16), (1, 32)), (0, 3, 16, 2.0))
    sens_state = gaussian(seeds[1], (SATS, SEGS, M, S), 0.1, 0.59765625, ((0, 16), (1, 32)))
    misfit = gaussian(seeds[2], (SATS, SEGS, M), 1.0, 6.0, ((0, 16), (1, 32)), jnp.float32)
    depth = jnp.clip(0.2 + 0.7 * jax.random.uniform(seeds[3], (SATS, SEGS, M), jnp.float32) ** level_of(seeds[3], (SATS, SEGS, M), ((0, 16), (1, 32)), -0.2, 0.2), 0.2, 0.9)
    cycle_count = draw_cycle_count(jax.random.fold_in(seeds[10], 71), 0)
    node_side = draw_node_side(jax.random.fold_in(seeds[10], 71), 0)
    transition = gaussian(seeds[6], (SATS, SEGS, S, S), S ** -0.5, 0.75, ((0, 16), (1, 32)))
    cont_sens = gaussian(seeds[7], (SATS, SEGS, S, P_SIZE), 0.1, 0.59765625, ((0, 16), (1, 32)))
    noise_root = gaussian(seeds[8], (SATS, SEGS, S, S), 0.0625, 0.4, ((0, 16), (1, 32)), jnp.float32)
    cont_misfit = gaussian(seeds[9], (SATS, SEGS, S), 1.0, 6.0, ((0, 16), (1, 32)), jnp.float32)
    return {"sens_params": sens_params, "sens_state": sens_state, "misfit": misfit, "depth": depth, "cycle_count": cycle_count, "node_side": node_side, "transition": transition, "cont_sens": cont_sens, "noise_root": noise_root, "cont_misfit": cont_misfit}


highest = lax.Precision.HIGHEST

def pick_segment(array, index):
    return lax.dynamic_index_in_dim(array, index, axis=1, keepdims=False)

def reference(sens_params, sens_state, misfit, depth, cycle_count, node_side, transition, cont_sens, noise_root, cont_misfit):
    positions = jnp.arange(M, dtype=jnp.int32)
    live_mask = (positions[None, None, :] < cycle_count[:, :, None]).astype(jnp.float32)
    used_depth = live_mask * depth
    through = lax.optimization_barrier(jnp.sum(used_depth, axis=2))
    prior_age = jnp.cumsum(through, axis=1) - through
    inner_age = jnp.cumsum(used_depth, axis=2) - used_depth
    age_scale = 4.0 / (M * SEGS)
    weights = live_mask / (1.0 + (prior_age[:, :, None] + inner_age) * age_scale)
    root_weight = jnp.sqrt(weights)
    eye_block = jnp.eye(S, dtype=jnp.float32)

    def one_segment(carry, index):
        gram_acc, grad_acc = carry
        root_seg = pick_segment(root_weight, index)
        weighted_sens = (root_seg[:, :, None] * pick_segment(sens_params, index).astype(jnp.float32)).astype(jnp.bfloat16)
        weighted_res = (root_seg * pick_segment(misfit, index)).astype(jnp.bfloat16)
        side = pick_segment(node_side, index).astype(jnp.float32)[:, :, None]
        state_rows = root_seg[:, :, None] * pick_segment(sens_state, index).astype(jnp.float32)
        state_pair = jnp.concatenate([state_rows * (1.0 - side), state_rows * side], axis=2).astype(jnp.bfloat16)
        live_link = (index < SEGS - 1).astype(jnp.float32)
        root_info = (eye_block[None] + pick_segment(noise_root, index)) * live_link
        state_map = jnp.einsum('sab,sbc->sac', root_info, pick_segment(transition, index).astype(jnp.float32), precision=highest)
        param_map = jnp.einsum('sab,sbp->sap', root_info, pick_segment(cont_sens, index).astype(jnp.float32), precision=highest).astype(jnp.bfloat16)
        cont_res = jnp.einsum('sab,sb->sa', root_info, pick_segment(cont_misfit, index), precision=highest).astype(jnp.bfloat16)
        stacked = jnp.concatenate([weighted_sens, param_map], axis=1).reshape(-1, P_SIZE)
        res_vec = jnp.concatenate([weighted_res, -cont_res], axis=1).reshape(-1)
        gram_acc = gram_acc + jnp.dot(stacked.T, stacked, preferred_element_type=jnp.float32)
        grad_acc = grad_acc + jnp.dot(res_vec, stacked, preferred_element_type=jnp.float32)
        pair_f = state_pair.astype(jnp.float32)
        sens_f = weighted_sens.astype(jnp.float32)
        pair_gram = jnp.einsum('smi,smk->sik', pair_f, pair_f)
        pair_cross = jnp.einsum('smi,smp->sip', pair_f, sens_f)
        pair_grad = jnp.einsum('smi,sm->si', pair_f, weighted_res.astype(jnp.float32))
        map_f = param_map.astype(jnp.float32)
        res_f = cont_res.astype(jnp.float32)
        own_hess = pair_gram[:, :S, :S] + jnp.einsum('sai,saj->sij', state_map, state_map, precision=highest)
        own_cross = pair_cross[:, :S] + jnp.einsum('sai,sap->sip', state_map, map_f, precision=highest)
        own_grad = pair_grad[:, :S] - jnp.einsum('sai,sa->si', state_map, res_f, precision=highest)
        next_hess = pair_gram[:, S:, S:] + jnp.einsum('sai,saj->sij', root_info, root_info, precision=highest)
        next_cross = pair_cross[:, S:] - jnp.einsum('sai,sap->sip', root_info, map_f, precision=highest)
        next_grad = pair_grad[:, S:] + jnp.einsum('sai,sa->si', root_info, res_f, precision=highest)
        coupling = -jnp.einsum('sai,saj->sij', state_map, root_info, precision=highest)
        return ((gram_acc, grad_acc), (own_hess, own_cross, own_grad, next_hess, next_cross, next_grad, coupling))
    start = (jnp.zeros((P_SIZE, P_SIZE), jnp.float32), jnp.zeros((P_SIZE,), jnp.float32))
    (gram_acc, grad_acc), blocks = lax.scan(one_segment, start, jnp.arange(SEGS, dtype=jnp.int32))
    own_hess, own_cross, own_grad, next_hess, next_cross, next_grad, coupling = blocks

    def moved(values):
        return jnp.concatenate([jnp.zeros_like(values[:1]), values[:-1]], axis=0)
    node_hess = jnp.swapaxes(own_hess + moved(next_hess), 0, 1)
    node_cross = jnp.swapaxes(own_cross + moved(next_cross), 0, 1)
    node_grad = jnp.swapaxes(own_grad + moved(next_grad), 0, 1)
    node_coupling = jnp.swapaxes(coupling, 0, 1)
    norm_factor = 1.0 / (SATS * SEGS)
    return (gram_acc * norm_factor, grad_acc * norm_factor, node_hess, node_cross, node_grad, node_coupling)
```

```python
import jax
import jax.numpy as jnp
from jax import lax
from jax.experimental import pallas as pl
from jax.experimental.pallas import tpu as pltpu
from jax.sharding import PartitionSpec as P

highest = lax.Precision.HIGHEST
MESH = pl.DeviceIdType.MESH
F32 = jnp.float32
BF16 = jnp.bfloat16

NX, NY, NZ = 4, 8, 8
M, S, PS = 320, 64, 1024
COLS = PS // NX
HALF = NZ // 2 * 64


def dot0(a, b, precision=None):
    return lax.dot_general(
        a, b, (((0,), (0,)), ((), ())), precision=precision, preferred_element_type=F32
    )


def kernel(
    sp, ss, mis, dep, cc, side, tr, cs, nr, cm,
    gram, grad, hess, cross, ngrad, coup,
    A, G2, R0, RX1, RX2, W, RY, V, RZ, FIN,
    TX, TY, GC, GX, GY, GZ, HB, HC, HBr, HCr,
    tx_s, tx_r, ty_s, ty_r, core_s, core_r, x1_s, x1_r, x2_s, x2_r,
    y_s, y_r, z_s, z_r, ay_s, ay_r, ax_s, ax_r,
    gc_s, gc_r, gx_s, gx_r, gy_s, gy_r, gz_s, gz_r, h_s, h_r,
):
    sat = lax.axis_index("sat")
    seg = lax.axis_index("seg")
    z, c = sat // 2, sat % 2
    y, x = seg // NX, seg % NX

    core_dev = (sat + 1 - 2 * c, seg)

    def x_dev(k):
        return (sat, y * NX + (x + k) % NX)

    def y_dev(k):
        return (sat, ((y + k) % NY) * NX + x)

    def z_dev(k):
        return (((z + k) % NZ) * 2 + c, seg)

    after = (sat, (seg + 1) % (NX * NY))
    before = (sat, (seg + NX * NY - 1) % (NX * NY))

    def copy(src, dst, send, recv, dev):
        return pltpu.make_async_remote_copy(
            src_ref=src, dst_ref=dst, send_sem=send, recv_sem=recv,
            device_id=dev, device_id_type=MESH,
        )

    barrier = pltpu.get_barrier_semaphore()
    partners = [core_dev, after, before]
    partners += [x_dev(k) for k in range(1, NX)]
    partners += [y_dev(k) for k in range(1, NY)]
    partners += [z_dev(k) for k in range(1, NZ)]
    for dev in partners:
        pl.semaphore_signal(barrier, inc=1, device_id=dev, device_id_type=MESH)

    rows = lax.broadcasted_iota(jnp.int32, (M, M), 0)
    lanes = lax.broadcasted_iota(jnp.int32, (M, M), 1)
    count = cc[...]
    used = jnp.where(lax.broadcasted_iota(jnp.int32, (1, M), 1) < count, dep[...], 0.0)
    through = jnp.sum(used, axis=1, keepdims=True)
    TX[x] = jnp.broadcast_to(through, (1, 128))

    pl.semaphore_wait(barrier, len(partners))

    def tx(k):
        return copy(TX.at[x], TX.at[x], tx_s.at[k - 1], tx_r.at[k - 1], x_dev(k))

    for k in range(1, NX):
        tx(k).start()

    link = jnp.where(seg < NX * NY - 1, 1.0, 0.0).astype(F32)
    r64 = lax.broadcasted_iota(jnp.int32, (S, S), 0)
    l64 = lax.broadcasted_iota(jnp.int32, (S, S), 1)
    root = (jnp.where(r64 == l64, 1.0, 0.0) + nr[...]) * link
    pm = jnp.dot(
        root, cs[...].astype(F32), precision=highest, preferred_element_type=F32
    ).astype(BF16)
    A[M:, :] = pm
    inner = jnp.sum(jnp.where(lanes < rows, used, 0.0), axis=1, keepdims=True)

    for k in range(1, NX):
        tx(k).wait_recv()
    xprior = jnp.zeros((1, 128), F32)
    total = jnp.zeros((1, 128), F32)
    for k in range(NX):
        part = TX[k]
        total = total + part
        xprior = xprior + jnp.where(k < x, part, 0.0)
    TY[y] = total

    def ty(k):
        return copy(TY.at[y], TY.at[y], ty_s.at[k - 1], ty_r.at[k - 1], y_dev(k))

    for k in range(1, NY):
        ty(k).start()

    smap = jnp.dot(
        root, tr[...].astype(F32), precision=highest, preferred_element_type=F32
    )
    both = jnp.concatenate([smap, root], axis=1)
    small = dot0(both, both, highest)
    wide = dot0(both, pm.astype(F32), highest)
    coup[...] = -small[:S, S:]
    cres = jnp.sum(root * cm[...], axis=1, keepdims=True).astype(BF16).astype(F32)
    cres_row = jnp.sum(jnp.where(r64 == l64, cres, 0.0), axis=0, keepdims=True)
    state_grad = jnp.sum(both * cres, axis=0, keepdims=True)
    side_f = side[...].astype(F32)
    side_col = jnp.sum(jnp.where(rows == lanes, side_f, 0.0), axis=1, keepdims=True)
    live_col = jnp.where(
        lax.broadcasted_iota(jnp.int32, (M, 1), 0) < count, 1.0, 0.0
    ).astype(F32)

    for k in range(1, NY):
        ty(k).wait_recv()
    prior = xprior
    for k in range(NY):
        prior = prior + jnp.where(k < y, TY[k], 0.0)

    age = inner + prior[:, 0:1]
    weight = jnp.sqrt(live_col / (1.0 + age * (4.0 / (M * NX * NY))))
    weight_row = jnp.sum(jnp.where(rows == lanes, weight, 0.0), axis=0, keepdims=True)
    A[:M, :] = (weight * sp[...].astype(F32)).astype(BF16)
    state_rows = weight * ss[...].astype(F32)
    pair = jnp.concatenate(
        [state_rows * (1.0 - side_col), state_rows * side_col], axis=1
    ).astype(BF16)
    res8 = jnp.broadcast_to(weight_row * mis[...], (8, M)).astype(BF16)
    cres8 = jnp.broadcast_to(cres_row, (8, S)).astype(BF16)
    ws = A[:M, :]

    pgram = dot0(pair, pair)
    pcross = dot0(pair, ws)
    pgrad = jnp.dot(res8, pair, preferred_element_type=F32)[0:1]
    HC[...] = pcross[S:] - wide[S:]
    HB[...] = jnp.zeros_like(HB)
    HB[0:S, 0:S] = pgram[S:, S:] + small[S:, S:]
    HB[S : S + 1, 0:S] = pgrad[:, S:] + state_grad[:, S:]

    halo = [
        copy(HC, HCr, h_s.at[0], h_r.at[0], after),
        copy(HB, HBr, h_s.at[1], h_r.at[1], after),
    ]

    @pl.when(seg < NX * NY - 1)
    def _():
        for h in halo:
            h.start()

    cross[...] = pcross[:S] + wide[:S]
    hess[...] = pgram[:S, :S] + small[:S, :S]
    ngrad[...] = pgrad[:, :S] - state_grad[:, :S]

    def core_copy(zi):
        part = pl.ds(pl.multiple_of(zi * 64, 64), 64)
        return copy(
            G2.at[1 - c, :, part, :], R0.at[:, part, :], core_s.at[zi], core_r.at[zi], core_dev
        )

    def gram_step(i, _):
        zi = (i % 2) * (NZ // 2) + i // 2
        g = dot0(A[:, pl.ds(pl.multiple_of(zi * 128, 128), 128)], A[...])
        part = pl.ds(pl.multiple_of(zi * 64, 64), 64)
        for q in range(NX):
            G2[0, q, part, :] = g[:64, q * COLS : (q + 1) * COLS]
            G2[1, q, part, :] = g[64:, q * COLS : (q + 1) * COLS]
        core_copy(zi).start()
        return 0

    lax.fori_loop(0, NZ, gram_step, 0)

    GC[0] = (
        jnp.dot(res8, ws, preferred_element_type=F32)
        - jnp.dot(cres8, pm, preferred_element_type=F32)
    )[0:1]
    gc = copy(GC.at[0], GC.at[1], gc_s, gc_r, core_dev)
    gc.start()

    far, right, left = (x + 2) % NX, (x + 1) % NX, (x + 3) % NX

    def rows64(j):
        return pl.ds(pl.multiple_of(j * 64, 64), 64)

    def x1(d, j):
        zi = d * (NZ // 2) + j
        return copy(
            R0.at[far, rows64(zi), :], RX1.at[d, rows64(j), :],
            x1_s.at[d, j], x1_r.at[d, j], x_dev(1 if d == 0 else 3),
        )

    def x2(d, zi):
        return copy(
            R0.at[right if d == 0 else left, rows64(zi), :], RX2.at[d, rows64(zi), :],
            x2_s.at[d, zi], x2_r.at[d, zi], x_dev(1 if d == 0 else 3),
        )

    def x_first(j, _):
        for d in range(2):
            zi = d * (NZ // 2) + j
            core_copy(zi).wait_recv()
            R0[:, rows64(zi), :] = R0[:, rows64(zi), :] + G2[c, :, rows64(zi), :]
            x1(d, j).start()
        for d in range(2):
            x2(1 - d, d * (NZ // 2) + j).start()
        return 0

    lax.fori_loop(0, NZ // 2, x_first, 0)

    gc.wait_recv()
    GX[x] = GC[0] + GC[1]

    def gx(k):
        return copy(GX.at[x], GX.at[x], gx_s.at[k - 1], gx_r.at[k - 1], x_dev(k))

    for k in range(1, NX):
        gx(k).start()

    def x_second(j, _):
        for d in range(2):
            zi = d * (NZ // 2) + j
            dest = right if d == 0 else left
            x1(d, j).wait_recv()
            R0[dest, rows64(zi), :] = R0[dest, rows64(zi), :] + RX1[d, rows64(j), :]
            x2(d, zi).start()
        return 0

    lax.fori_loop(0, NZ // 2, x_second, 0)

    for k in range(1, NX):
        gx(k).wait_recv()
    GY[y] = (GX[0] + GX[1]) + (GX[2] + GX[3])

    def gy(k):
        return copy(GY.at[y], GY.at[y], gy_s.at[k - 1], gy_r.at[k - 1], y_dev(k))

    for k in range(1, NY):
        gy(k).start()

    def x_last(i, _):
        zi = (i % 2) * (NZ // 2) + i // 2
        for d in range(2):
            x2(d, zi).wait_recv()
        own = R0[x, rows64(zi), :] + RX2[0, rows64(zi), :] + RX2[1, rows64(zi), :]
        W[:, zi] = own.reshape(NY, 8, COLS)
        return 0

    lax.fori_loop(0, NZ, x_last, 0)

    def yc(k):
        return copy(W.at[(y + k) % NY], RY.at[k - 1], y_s.at[k - 1], y_r.at[k - 1], y_dev(k))

    for k in range(1, NY):
        yc(k).start()
    for k in range(1, NY):
        gy(k).wait_recv()
    part = GY[0]
    for k in range(1, NY):
        part = part + GY[k]
    GZ[z] = part

    def gz(k):
        return copy(GZ.at[z], GZ.at[z], gz_s.at[k - 1], gz_r.at[k - 1], z_dev(k))

    for k in range(1, NZ):
        gz(k).start()

    @pl.when(seg > 0)
    def _():
        for h in halo:
            h.wait_recv()
        cross[...] = cross[...] + HCr[...]
        hess[...] = hess[...] + HBr[0:S, 0:S]
        ngrad[...] = ngrad[...] + HBr[S : S + 1, 0:S]

    V[...] = W[y]
    for k in range(1, NY):
        yc(k).wait_recv()
        V[...] = V[...] + RY[k - 1]

    def zc(k):
        return copy(V.at[(z + k) % NZ], RZ.at[k - 1], z_s.at[k - 1], z_r.at[k - 1], z_dev(k))

    for k in range(1, NZ):
        zc(k).start()
    for k in range(1, NZ):
        gz(k).wait_recv()
    part = GZ[0]
    for k in range(1, NZ):
        part = part + GZ[k]
    scale = 1.0 / (2 * NX * NY * NZ)
    grad[...] = part * scale

    own = V[z]
    for k in range(1, NZ):
        zc(k).wait_recv()
        own = own + RZ[k - 1]
    FIN[x, y] = own * scale

    def ay(k):
        return copy(FIN.at[x, y], FIN.at[x, y], ay_s.at[k - 1], ay_r.at[k - 1], y_dev(k))

    for k in range(1, NY):
        ay(k).start()
    for k in range(1, NY):
        ay(k).wait_recv()

    def ax(k):
        return copy(FIN.at[x], FIN.at[x], ax_s.at[k - 1], ax_r.at[k - 1], x_dev(k))

    for k in range(1, NX):
        ax(k).start()
    for k in range(1, NX):
        ax(k).wait_recv()
    for q in range(NX):
        gram[:, q * COLS : (q + 1) * COLS] = FIN[q].reshape(64, COLS)

    for k in range(1, NX):
        tx(k).wait_send()
        gx(k).wait_send()
        ax(k).wait_send()
    for k in range(1, NY):
        ty(k).wait_send()
        gy(k).wait_send()
        yc(k).wait_send()
        ay(k).wait_send()
    for k in range(1, NZ):
        gz(k).wait_send()
        zc(k).wait_send()
    gc.wait_send()

    def drain(zi, _):
        core_copy(zi).wait_send()
        for d in range(2):
            x2(d, zi).wait_send()
        return 0

    lax.fori_loop(0, NZ, drain, 0)

    def drain1(j, _):
        for d in range(2):
            x1(d, j).wait_send()
        return 0

    lax.fori_loop(0, NZ // 2, drain1, 0)

    @pl.when(seg < NX * NY - 1)
    def _():
        for h in halo:
            h.wait_send()


def shards(sp, ss, mis, dep, cc, side, tr, cs, nr, cm):
    vmem = pl.BlockSpec(memory_space=pltpu.VMEM)
    sem = pltpu.SemaphoreType.DMA
    shapes = [(64, PS), (1, PS), (S, S), (S, PS), (1, S), (S, S)]
    outs = pl.pallas_call(
        kernel,
        out_shape=[jax.ShapeDtypeStruct(s, F32) for s in shapes],
        in_specs=[vmem] * 10,
        out_specs=[vmem] * 6,
        scratch_shapes=[
            pltpu.VMEM((M + S, PS), BF16),
            pltpu.VMEM((2, NX, 512, COLS), F32),
            pltpu.VMEM((NX, 512, COLS), F32),
            pltpu.VMEM((2, HALF, COLS), F32),
            pltpu.VMEM((2, 512, COLS), F32),
            pltpu.VMEM((NY, NZ, 8, COLS), F32),
            pltpu.VMEM((NY - 1, NZ, 8, COLS), F32),
            pltpu.VMEM((NZ, 8, COLS), F32),
            pltpu.VMEM((NZ - 1, 8, COLS), F32),
            pltpu.VMEM((NX, NY, 8, COLS), F32),
            pltpu.VMEM((NX, 1, 128), F32),
            pltpu.VMEM((NY, 1, 128), F32),
            pltpu.VMEM((2, 1, PS), F32),
            pltpu.VMEM((NX, 1, PS), F32),
            pltpu.VMEM((NY, 1, PS), F32),
            pltpu.VMEM((NZ, 1, PS), F32),
            pltpu.VMEM((72, 128), F32),
            pltpu.VMEM((S, PS), F32),
            pltpu.VMEM((72, 128), F32),
            pltpu.VMEM((S, PS), F32),
            sem((NX - 1,)), sem((NX - 1,)),
            sem((NY - 1,)), sem((NY - 1,)),
            sem((NZ,)), sem((NZ,)),
            sem((2, NZ // 2)), sem((2, NZ // 2)),
            sem((2, NZ)), sem((2, NZ)),
            sem((NY - 1,)), sem((NY - 1,)),
            sem((NZ - 1,)), sem((NZ - 1,)),
            sem((NY - 1,)), sem((NY - 1,)),
            sem((NX - 1,)), sem((NX - 1,)),
            sem, sem,
            sem((NX - 1,)), sem((NX - 1,)),
            sem((NY - 1,)), sem((NY - 1,)),
            sem((NZ - 1,)), sem((NZ - 1,)),
            sem((2,)), sem((2,)),
        ],
        compiler_params=pltpu.CompilerParams(
            collective_id=0, has_side_effects=True, vmem_limit_bytes=48 * 1024 * 1024
        ),
    )(
        sp.reshape(M, PS), ss.reshape(M, S), mis.reshape(1, M), dep.reshape(1, M), cc,
        side.reshape(1, M), tr.reshape(S, S), cs.reshape(S, PS), nr.reshape(S, S),
        cm.reshape(1, S),
    )
    gram, grad, hess, cross, ngrad, coup = outs
    return (
        gram, grad.reshape(PS), hess.reshape(1, 1, S, S), cross.reshape(1, 1, S, PS),
        ngrad.reshape(1, 1, S), coup.reshape(1, 1, S, S),
    )


def solution(mesh):
    wide = P("sat", "seg", None, None)
    line = P("sat", "seg", None)
    return jax.shard_map(
        shards,
        mesh=mesh,
        in_specs=(wide, wide, line, line, P("sat", "seg"), line, wide, wide, wide, line),
        out_specs=(P("sat", None), P(), wide, wide, line, wide),
        check_vma=False,
    )
```

```python
import jax
import jax.numpy as jnp
from jax import lax
from jax.experimental import pallas as pl
from jax.experimental.pallas import tpu as pltpu
from jax.sharding import PartitionSpec as P

highest = lax.Precision.HIGHEST
MESH = pl.DeviceIdType.MESH
F32 = jnp.float32
BF16 = jnp.bfloat16

NX, NY, NZ = 4, 8, 8
M, S, PS = 320, 64, 1024
VMEM_ALL = 67043328
OUTS = [(64, PS), (1, PS), (S, S), (S, PS), (1, S), (S, S)]
COLS = PS // NX
HALF = NZ // 2 * 64


def dot0(a, b, precision=None):
    return lax.dot_general(
        a, b, (((0,), (0,)), ((), ())), precision=precision, preferred_element_type=F32
    )


def dot1(a, b):
    return lax.dot_general(a, b, (((1,), (1,)), ((), ())), preferred_element_type=F32)


def kernel(
    sp_h, ss_h, mis_h, dep_h, cc, side_h, tr_h, cs_h, nr_h, cm_h,
    gram_h, grad_h, hess_h, cross_h, ngrad_h, coup_h,
    gram, grad, hess, cross, ngrad, coup, out_s,
    sp, ss, mis, dep, side, tr, cs, nr, cm, in_s,
    A, G2, R0, RX1, RX2, W, R1, V, R2, FA, FB,
    TX, TY, GC, GX, GY, GZ, HB, HC, HBr, HCr,
    tx_s, tx_r, ty_s, ty_r, core_s, core_r, x1_s, x1_r, x2_s, x2_r,
    p_s, p_r, q_s, q_r, ay_s, ay_r, ax_s, ax_r,
    gc_s, gc_r, gx_s, gx_r, gy_s, gy_r, gz_s, gz_r, h_s, h_r,
):
    sat = lax.axis_index("sat")
    seg = lax.axis_index("seg")
    z, c = sat // 2, sat % 2
    y, x = seg // NX, seg % NX

    core_dev = (sat + 1 - 2 * c, seg)

    def x_dev(k):
        return (sat, y * NX + (x + k) % NX)

    def y_dev(k):
        return (sat, ((y + k) % NY) * NX + x)

    def z_dev(k):
        return (((z + k) % NZ) * 2 + c, seg)

    after = (sat, (seg + 1) % (NX * NY))
    before = (sat, (seg + NX * NY - 1) % (NX * NY))

    def copy(src, dst, send, recv, dev):
        return pltpu.make_async_remote_copy(
            src_ref=src, dst_ref=dst, send_sem=send, recv_sem=recv,
            device_id=dev, device_id_type=MESH,
        )

    loads = [
        pltpu.make_async_copy(a, b, in_s.at[i])
        for i, (a, b) in enumerate(
            [
                (dep_h, dep), (nr_h, nr), (cs_h, cs), (tr_h, tr), (cm_h, cm),
                (mis_h, mis), (side_h, side), (ss_h, ss), (sp_h, sp),
            ]
        )
    ]
    for load in loads:
        load.start()
    results = [
        pltpu.make_async_copy(a, b, out_s.at[i])
        for i, (a, b) in enumerate(
            [
                (gram, gram_h), (grad, grad_h), (hess, hess_h),
                (cross, cross_h), (ngrad, ngrad_h), (coup, coup_h),
            ]
        )
    ]
    barrier = pltpu.get_barrier_semaphore()
    partners = [core_dev, after, before]
    partners += [x_dev(k) for k in range(1, NX)]
    partners += [y_dev(k) for k in range(1, NY)]
    partners += [z_dev(k) for k in range(1, NZ)]
    for dev in partners:
        pl.semaphore_signal(barrier, inc=1, device_id=dev, device_id_type=MESH)

    rows = lax.broadcasted_iota(jnp.int32, (M, M), 0)
    lanes = lax.broadcasted_iota(jnp.int32, (M, M), 1)
    count = cc[...]
    loads[0].wait()
    used = jnp.where(lax.broadcasted_iota(jnp.int32, (1, M), 1) < count, dep[...], 0.0)
    through = jnp.sum(used, axis=1, keepdims=True)
    TX[x] = jnp.broadcast_to(through, (1, 128))

    pl.semaphore_wait(barrier, len(partners))

    def tx(k):
        return copy(TX.at[x], TX.at[x], tx_s.at[k - 1], tx_r.at[k - 1], x_dev(k))

    for k in range(1, NX):
        tx(k).start()

    link = jnp.where(seg < NX * NY - 1, 1.0, 0.0).astype(F32)
    r64 = lax.broadcasted_iota(jnp.int32, (S, S), 0)
    l64 = lax.broadcasted_iota(jnp.int32, (S, S), 1)
    for load in loads[1:]:
        load.wait()
    root = (jnp.where(r64 == l64, 1.0, 0.0) + nr[...]) * link
    pm = jnp.dot(
        root, cs[...].astype(F32), precision=highest, preferred_element_type=F32
    ).astype(BF16)
    A[M:, :] = pm
    inner = jnp.sum(jnp.where(lanes < rows, used, 0.0), axis=1, keepdims=True)

    for k in range(1, NX):
        tx(k).wait_recv()
    xprior = jnp.zeros((1, 128), F32)
    total = jnp.zeros((1, 128), F32)
    for k in range(NX):
        part = TX[k]
        total = total + part
        xprior = xprior + jnp.where(k < x, part, 0.0)
    TY[y] = total

    def ty(k):
        return copy(TY.at[y], TY.at[y], ty_s.at[k - 1], ty_r.at[k - 1], y_dev(k))

    for k in range(1, NY):
        ty(k).start()

    smap = jnp.dot(
        root, tr[...].astype(F32), precision=highest, preferred_element_type=F32
    )
    both = jnp.concatenate([smap, root], axis=1)
    small = dot0(both, both, highest)
    wide = dot0(both, pm.astype(F32), highest)
    coup[...] = -small[:S, S:]
    results[5].start()
    cres = jnp.sum(root * cm[...], axis=1, keepdims=True).astype(BF16).astype(F32)
    cres_row = jnp.sum(jnp.where(r64 == l64, cres, 0.0), axis=0, keepdims=True)
    state_grad = jnp.sum(both * cres, axis=0, keepdims=True)
    side_f = side[...].astype(F32)
    live_col = jnp.where(
        lax.broadcasted_iota(jnp.int32, (M, 1), 0) < count, 1.0, 0.0
    ).astype(F32)

    for k in range(1, NY):
        ty(k).wait_recv()
    prior = xprior
    for k in range(NY):
        prior = prior + jnp.where(k < y, TY[k], 0.0)

    age = inner + prior[:, 0:1]
    weight = jnp.sqrt(live_col / (1.0 + age * (4.0 / (M * NX * NY))))
    weight_row = jnp.sum(jnp.where(rows == lanes, weight, 0.0), axis=0, keepdims=True)
    A[:M, :] = (weight * sp[...].astype(F32)).astype(BF16)
    res8 = jnp.broadcast_to(weight_row * mis[...], (8, M)).astype(BF16)
    cres8 = jnp.broadcast_to(cres_row, (8, S)).astype(BF16)

    def core_copy(zi):
        part = pl.ds(pl.multiple_of(zi * 64, 64), 64)
        return copy(
            G2.at[1 - c, :, part, :], R0.at[:, part, :], core_s.at[zi], core_r.at[zi], core_dev
        )

    def gram_step(i, _):
        zi = (i % 2) * (NZ // 2) + i // 2
        g = dot0(A[:, pl.ds(pl.multiple_of(zi * 128, 128), 128)], A[...])
        part = pl.ds(pl.multiple_of(zi * 64, 64), 64)
        for q in range(NX):
            G2[0, q, part, :] = g[:64, q * COLS : (q + 1) * COLS]
            G2[1, q, part, :] = g[64:, q * COLS : (q + 1) * COLS]
        core_copy(zi).start()
        return 0

    lax.fori_loop(0, NZ, gram_step, 0)

    GC[0] = (
        jnp.dot(res8, A[:M, :], preferred_element_type=F32)
        - jnp.dot(cres8, pm, preferred_element_type=F32)
    )[0:1]
    gc = copy(GC.at[0], GC.at[1], gc_s, gc_r, core_dev)
    gc.start()

    far, right, left = (x + 2) % NX, (x + 1) % NX, (x + 3) % NX

    def rows64(j):
        return pl.ds(pl.multiple_of(j * 64, 64), 64)

    def x1(d, j):
        zi = d * (NZ // 2) + j
        return copy(
            R0.at[far, rows64(zi), :], RX1.at[d, rows64(j), :],
            x1_s.at[d, j], x1_r.at[d, j], x_dev(1 if d == 0 else 3),
        )

    def x2(d, zi):
        return copy(
            R0.at[right if d == 0 else left, rows64(zi), :], RX2.at[d, rows64(zi), :],
            x2_s.at[d, zi], x2_r.at[d, zi], x_dev(1 if d == 0 else 3),
        )

    def x_first(j, _):
        for d in range(2):
            zi = d * (NZ // 2) + j
            core_copy(zi).wait_recv()
            R0[:, rows64(zi), :] = R0[:, rows64(zi), :] + G2[c, :, rows64(zi), :]
            x1(d, j).start()
        for d in range(2):
            x2(1 - d, d * (NZ // 2) + j).start()
        return 0

    lax.fori_loop(0, NZ // 2, x_first, 0)

    gc.wait_recv()
    GX[x] = GC[0] + GC[1]

    def gx(k):
        return copy(GX.at[x], GX.at[x], gx_s.at[k - 1], gx_r.at[k - 1], x_dev(k))

    for k in range(1, NX):
        gx(k).start()

    state_rows = weight_row * ss[...].astype(F32)
    pair = jnp.concatenate(
        [state_rows * (1.0 - side_f), state_rows * side_f], axis=0
    ).astype(BF16)
    pgram = dot1(pair, pair)
    pcross = jnp.dot(pair, A[:M, :], preferred_element_type=F32)
    pgrad = dot1(res8, pair)[0:1]
    HC[...] = pcross[S:] - wide[S:]
    HB[...] = jnp.zeros_like(HB)
    HB[0:S, 0:S] = pgram[S:, S:] + small[S:, S:]
    HB[S : S + 1, 0:S] = pgrad[:, S:] + state_grad[:, S:]
    cross[...] = pcross[:S] + wide[:S]
    hess[...] = pgram[:S, :S] + small[:S, :S]
    ngrad[...] = pgrad[:, :S] - state_grad[:, :S]

    def x_second(j, _):
        for d in range(2):
            zi = d * (NZ // 2) + j
            dest = right if d == 0 else left
            x1(d, j).wait_recv()
            R0[dest, rows64(zi), :] = R0[dest, rows64(zi), :] + RX1[d, rows64(j), :]
            x2(d, zi).start()
        return 0

    lax.fori_loop(0, NZ // 2, x_second, 0)

    halo = [
        copy(HC, HCr, h_s.at[0], h_r.at[0], after),
        copy(HB, HBr, h_s.at[1], h_r.at[1], after),
    ]

    @pl.when(seg < NX * NY - 1)
    def _():
        for h in halo:
            h.start()

    for k in range(1, NX):
        gx(k).wait_recv()
    GY[y] = (GX[0] + GX[1]) + (GX[2] + GX[3])

    def gy(k):
        return copy(GY.at[y], GY.at[y], gy_s.at[k - 1], gy_r.at[k - 1], y_dev(k))

    for k in range(1, NY):
        gy(k).start()

    def x_last(i, _):
        zi = (i % 2) * (NZ // 2) + i // 2
        for d in range(2):
            x2(d, zi).wait_recv()
        own = R0[x, rows64(zi), :] + RX2[0, rows64(zi), :] + RX2[1, rows64(zi), :]
        own = own.reshape(NY, 8, COLS)
        W[0, :, zi] = own[:, :, : COLS // 2]
        W[1, zi] = own[:, :, COLS // 2 :]
        return 0

    lax.fori_loop(0, NZ, x_last, 0)

    lines = [(y, y_dev, z, z_dev), (z, z_dev, y, y_dev)]

    def pc(g, k):
        at, dev, _, _ = lines[g]
        return copy(W.at[g, (at + k) % 8], R1.at[g, k - 1], p_s.at[g, k - 1], p_r.at[g, k - 1], dev(k))

    def qc(g, k):
        _, _, at, dev = lines[g]
        return copy(V.at[g, (at + k) % 8], R2.at[g, k - 1], q_s.at[g, k - 1], q_r.at[g, k - 1], dev(k))

    for k in range(1, 8):
        for g in range(2):
            pc(g, k).start()
    for k in range(1, NY):
        gy(k).wait_recv()
    part = GY[0]
    for k in range(1, NY):
        part = part + GY[k]
    GZ[z] = part

    def gz(k):
        return copy(GZ.at[z], GZ.at[z], gz_s.at[k - 1], gz_r.at[k - 1], z_dev(k))

    for k in range(1, NZ):
        gz(k).start()

    @pl.when(seg > 0)
    def _():
        for h in halo:
            h.wait_recv()
        cross[...] = cross[...] + HCr[...]
        hess[...] = hess[...] + HBr[0:S, 0:S]
        ngrad[...] = ngrad[...] + HBr[S : S + 1, 0:S]

    for i in (2, 3, 4):
        results[i].start()

    for g in range(2):
        acc = W[g, lines[g][0]]
        for k in range(1, 8):
            pc(g, k).wait_recv()
            acc = acc + R1[g, k - 1]
        V[g] = acc
        for k in range(1, 8):
            qc(g, k).start()
    for k in range(1, NZ):
        gz(k).wait_recv()
    part = GZ[0]
    for k in range(1, NZ):
        part = part + GZ[k]
    scale = 1.0 / (2 * NX * NY * NZ)
    grad[...] = part * scale
    results[1].start()

    done = []
    for g in range(2):
        own = V[g, lines[g][2]]
        for k in range(1, 8):
            qc(g, k).wait_recv()
            own = own + R2[g, k - 1]
        done.append(own * scale)
    FA[x, y] = done[0]
    FB[y, x] = done[1]

    def ay(g, k):
        block = FA.at[x, y] if g == 0 else FB.at[y]
        return copy(block, block, ay_s.at[g, k - 1], ay_r.at[g, k - 1], y_dev(k))

    def ax(g, k):
        block = FA.at[x] if g == 0 else FB.at[y, x]
        return copy(block, block, ax_s.at[g, k - 1], ax_r.at[g, k - 1], x_dev(k))

    for k in range(1, NY):
        ay(0, k).start()
    for k in range(1, NX):
        ax(1, k).start()
    for k in range(1, NX):
        ax(1, k).wait_recv()
    for k in range(1, NY):
        ay(1, k).start()
    for k in range(1, NY):
        ay(0, k).wait_recv()
    for k in range(1, NX):
        ax(0, k).start()
    for k in range(1, NY):
        ay(1, k).wait_recv()
    for q in range(NX):
        at = q * COLS + COLS // 2
        gram[:, at : at + COLS // 2] = FB[:, q].reshape(64, COLS // 2)
    for k in range(1, NX):
        ax(0, k).wait_recv()
    for q in range(NX):
        gram[:, q * COLS : q * COLS + COLS // 2] = FA[q].reshape(64, COLS // 2)

    results[0].start()

    for k in range(1, NX):
        tx(k).wait_send()
        gx(k).wait_send()
        for g in range(2):
            ax(g, k).wait_send()
    for k in range(1, NY):
        ty(k).wait_send()
        gy(k).wait_send()
        for g in range(2):
            ay(g, k).wait_send()
            pc(g, k).wait_send()
            qc(g, k).wait_send()
    for k in range(1, NZ):
        gz(k).wait_send()
    gc.wait_send()

    def drain(zi, _):
        core_copy(zi).wait_send()
        for d in range(2):
            x2(d, zi).wait_send()
        return 0

    lax.fori_loop(0, NZ, drain, 0)

    def drain1(j, _):
        for d in range(2):
            x1(d, j).wait_send()
        return 0

    lax.fori_loop(0, NZ // 2, drain1, 0)

    @pl.when(seg < NX * NY - 1)
    def _():
        for h in halo:
            h.wait_send()

    for out in results:
        out.wait()


def put_out(*refs):
    ins, outs, held, sems = refs[:6], refs[6:12], refs[12:18], refs[18]
    into = [pltpu.make_async_copy(ins[i], held[i], sems.at[0, i]) for i in range(6)]
    back = [pltpu.make_async_copy(held[i], outs[i], sems.at[1, i]) for i in range(6)]
    for one in into:
        one.start()
    for one, two in zip(into, back):
        one.wait()
        two.start()
    for two in back:
        two.wait()


def shards(sp, ss, mis, dep, cc, side, tr, cs, nr, cm):
    vmem = pl.BlockSpec(memory_space=pltpu.VMEM)
    hbm = pl.BlockSpec(memory_space=pltpu.HBM)
    sem = pltpu.SemaphoreType.DMA
    outs = pl.pallas_call(
        kernel,
        out_shape=[jax.ShapeDtypeStruct(s, F32) for s in OUTS],
        in_specs=[vmem if i == 4 else hbm for i in range(10)],
        out_specs=[hbm] * 6,
        scratch_shapes=[pltpu.VMEM(s, F32) for s in OUTS]
        + [
            sem((6,)),
            pltpu.VMEM((M, PS), BF16),
            pltpu.VMEM((S, M), BF16),
            pltpu.VMEM((1, M), F32),
            pltpu.VMEM((1, M), F32),
            pltpu.VMEM((1, M), jnp.int32),
            pltpu.VMEM((S, S), BF16),
            pltpu.VMEM((S, PS), BF16),
            pltpu.VMEM((S, S), F32),
            pltpu.VMEM((1, S), F32),
            sem((9,)),
            pltpu.VMEM((M + S, PS), BF16),
            pltpu.VMEM((2, NX, 512, COLS), F32),
            pltpu.VMEM((NX, 512, COLS), F32),
            pltpu.VMEM((2, HALF, COLS), F32),
            pltpu.VMEM((2, 512, COLS), F32),
            pltpu.VMEM((2, 8, 8, 8, COLS // 2), F32),
            pltpu.VMEM((2, 7, 8, 8, COLS // 2), F32),
            pltpu.VMEM((2, 8, 8, COLS // 2), F32),
            pltpu.VMEM((2, 7, 8, COLS // 2), F32),
            pltpu.VMEM((NX, NY, 8, COLS // 2), F32),
            pltpu.VMEM((NY, NX, 8, COLS // 2), F32),
            pltpu.VMEM((NX, 1, 128), F32),
            pltpu.VMEM((NY, 1, 128), F32),
            pltpu.VMEM((2, 1, PS), F32),
            pltpu.VMEM((NX, 1, PS), F32),
            pltpu.VMEM((NY, 1, PS), F32),
            pltpu.VMEM((NZ, 1, PS), F32),
            pltpu.VMEM((72, 128), F32),
            pltpu.VMEM((S, PS), F32),
            pltpu.VMEM((72, 128), F32),
            pltpu.VMEM((S, PS), F32),
            sem((NX - 1,)), sem((NX - 1,)),
            sem((NY - 1,)), sem((NY - 1,)),
            sem((NZ,)), sem((NZ,)),
            sem((2, NZ // 2)), sem((2, NZ // 2)),
            sem((2, NZ)), sem((2, NZ)),
            sem((2, 7)), sem((2, 7)),
            sem((2, 7)), sem((2, 7)),
            sem((2, NY - 1)), sem((2, NY - 1)),
            sem((2, NX - 1)), sem((2, NX - 1)),
            sem, sem,
            sem((NX - 1,)), sem((NX - 1,)),
            sem((NY - 1,)), sem((NY - 1,)),
            sem((NZ - 1,)), sem((NZ - 1,)),
            sem((2,)), sem((2,)),
        ],
        compiler_params=pltpu.CompilerParams(
            collective_id=0, has_side_effects=True, vmem_limit_bytes=VMEM_ALL
        ),
    )(
        sp.reshape(M, PS), ss.reshape(M, S).T, mis.reshape(1, M), dep.reshape(1, M), cc,
        side.reshape(1, M), tr.reshape(S, S), cs.reshape(S, PS), nr.reshape(S, S),
        cm.reshape(1, S),
    )
    outs = pl.pallas_call(
        put_out,
        out_shape=[jax.ShapeDtypeStruct(s, F32) for s in OUTS],
        in_specs=[hbm] * 6,
        out_specs=[hbm] * 6,
        scratch_shapes=[pltpu.VMEM(s, F32) for s in OUTS] + [sem((2, 6))],
        compiler_params=pltpu.CompilerParams(vmem_limit_bytes=VMEM_ALL),
    )(*outs)
    gram, grad, hess, cross, ngrad, coup = outs
    return (
        gram, grad.reshape(PS), hess.reshape(1, 1, S, S), cross.reshape(1, 1, S, PS),
        ngrad.reshape(1, 1, S), coup.reshape(1, 1, S, S),
    )


def solution(mesh):
    wide = P("sat", "seg", None, None)
    line = P("sat", "seg", None)
    return jax.shard_map(
        shards,
        mesh=mesh,
        in_specs=(wide, wide, line, line, P("sat", "seg"), line, wide, wide, wide, line),
        out_specs=(P("sat", None), P(), wide, wide, line, wide),
        check_vma=False,
    )
```

```python
import jax
import jax.numpy as jnp
from jax import lax
from jax.experimental import pallas as pl
from jax.experimental.pallas import tpu as pltpu
from jax.sharding import PartitionSpec as P

highest = lax.Precision.HIGHEST
MESH = pl.DeviceIdType.MESH
F32 = jnp.float32
BF16 = jnp.bfloat16

NX, NY, NZ = 4, 8, 8
M, S, PS = 320, 64, 1024
VMEM_ALL = 67043328
OUTS = [(64, PS), (1, PS), (S, S), (S, PS), (1, S), (S, S)]


def dot0(a, b, precision=None):
    return lax.dot_general(
        a, b, (((0,), (0,)), ((), ())), precision=precision, preferred_element_type=F32
    )


def dot1(a, b):
    return lax.dot_general(a, b, (((1,), (1,)), ((), ())), preferred_element_type=F32)


def kernel(
    sp_h, ss_h, mis_h, dep_h, cc, side_h, tr_h, cs_h, nr_h, cm_h,
    gram_h, grad_h, hess_h, cross_h, ngrad_h, coup_h,
    gram, grad, hess, cross, ngrad, coup, out_s,
    sp, ss, mis, dep, side, tr, cs, nr, cm, in_s,
    A, G2, R0, RX1, RX2, W, R1, V, R2, FA, FB, FAr, FBr,
    TX, TY, GC, GX, GY, GZ, HB, HC, HBr, HCr,
    tx_s, tx_r, ty_s, ty_r, core_s, core_r, x1_s, x1_r, x2_s, x2_r,
    p_s, p_r, q_s, q_r, fin_s, fin_r, ay_s, ay_r, ax_s, ax_r,
    gc_s, gc_r, gx_s, gx_r, gy_s, gy_r, gz_s, gz_r, h_s, h_r,
):
    sat = lax.axis_index("sat")
    seg = lax.axis_index("seg")
    z, c = sat // 2, sat % 2
    y, x = seg // NX, seg % NX

    core_dev = (sat + 1 - 2 * c, seg)

    def x_dev(k):
        return (sat, y * NX + (x + k) % NX)

    def y_dev(k):
        return (sat, ((y + k) % NY) * NX + x)

    def z_dev(k):
        return (((z + k) % NZ) * 2 + c, seg)

    after = (sat, (seg + 1) % (NX * NY))
    before = (sat, (seg + NX * NY - 1) % (NX * NY))

    def copy(src, dst, send, recv, dev):
        return pltpu.make_async_remote_copy(
            src_ref=src, dst_ref=dst, send_sem=send, recv_sem=recv,
            device_id=dev, device_id_type=MESH,
        )

    loads = [
        pltpu.make_async_copy(a, b, in_s.at[i])
        for i, (a, b) in enumerate(
            [
                (dep_h, dep), (nr_h, nr), (cs_h, cs), (tr_h, tr), (cm_h, cm),
                (mis_h, mis), (side_h, side), (ss_h, ss), (sp_h, sp),
            ]
        )
    ]
    for load in loads:
        load.start()
    results = [
        pltpu.make_async_copy(a, b, out_s.at[i])
        for i, (a, b) in enumerate(
            [
                (gram, gram_h), (grad, grad_h), (hess, hess_h),
                (cross, cross_h), (ngrad, ngrad_h), (coup, coup_h),
            ]
        )
    ]
    barrier = pltpu.get_barrier_semaphore()
    partners = [core_dev, after, before]
    partners += [x_dev(k) for k in range(1, NX)]
    partners += [y_dev(k) for k in range(1, NY)]
    partners += [z_dev(k) for k in range(1, NZ)]
    for dev in partners:
        pl.semaphore_signal(barrier, inc=1, device_id=dev, device_id_type=MESH)

    rows = lax.broadcasted_iota(jnp.int32, (M, M), 0)
    lanes = lax.broadcasted_iota(jnp.int32, (M, M), 1)
    count = cc[...]
    loads[0].wait()
    used = jnp.where(lax.broadcasted_iota(jnp.int32, (1, M), 1) < count, dep[...], 0.0)
    through = jnp.sum(used, axis=1, keepdims=True)
    TX[x] = jnp.broadcast_to(through, (1, 128))

    pl.semaphore_wait(barrier, len(partners))

    def tx(k):
        return copy(TX.at[x], TX.at[x], tx_s.at[k - 1], tx_r.at[k - 1], x_dev(k))

    for k in range(1, NX):
        tx(k).start()

    link = jnp.where(seg < NX * NY - 1, 1.0, 0.0).astype(F32)
    r64 = lax.broadcasted_iota(jnp.int32, (S, S), 0)
    l64 = lax.broadcasted_iota(jnp.int32, (S, S), 1)
    for load in loads[1:]:
        load.wait()
    root = (jnp.where(r64 == l64, 1.0, 0.0) + nr[...]) * link
    pm = jnp.dot(
        root, cs[...].astype(F32), precision=highest, preferred_element_type=F32
    ).astype(BF16)
    A[M:, :PS] = pm
    inner = jnp.sum(jnp.where(lanes < rows, used, 0.0), axis=1, keepdims=True)

    for k in range(1, NX):
        tx(k).wait_recv()
    xprior = jnp.zeros((1, 128), F32)
    total = jnp.zeros((1, 128), F32)
    for k in range(NX):
        part = TX[k]
        total = total + part
        xprior = xprior + jnp.where(k < x, part, 0.0)
    TY[y] = total

    def ty(k):
        return copy(TY.at[y], TY.at[y], ty_s.at[k - 1], ty_r.at[k - 1], y_dev(k))

    for k in range(1, NY):
        ty(k).start()

    smap = jnp.dot(
        root, tr[...].astype(F32), precision=highest, preferred_element_type=F32
    )
    both = jnp.concatenate([smap, root], axis=1)
    small = dot0(both, both, highest)
    wide = dot0(both, pm.astype(F32), highest)
    coup[...] = -small[:S, S:]
    results[5].start()
    cres = jnp.sum(root * cm[...], axis=1, keepdims=True).astype(BF16).astype(F32)
    cres_row = jnp.sum(jnp.where(r64 == l64, cres, 0.0), axis=0, keepdims=True)
    state_grad = jnp.sum(both * cres, axis=0, keepdims=True)
    side_f = side[...].astype(F32)
    live_col = jnp.where(
        lax.broadcasted_iota(jnp.int32, (M, 1), 0) < count, 1.0, 0.0
    ).astype(F32)

    for k in range(1, NY):
        ty(k).wait_recv()
    prior = xprior
    for k in range(NY):
        prior = prior + jnp.where(k < y, TY[k], 0.0)

    age = inner + prior[:, 0:1]
    weight = jnp.sqrt(live_col / (1.0 + age * (4.0 / (M * NX * NY))))
    weight_row = jnp.sum(jnp.where(rows == lanes, weight, 0.0), axis=0, keepdims=True)
    A[:M, :PS] = (weight * sp[...].astype(F32)).astype(BF16)
    A[:, PS:] = A[:, : PS // 2]
    res8 = jnp.broadcast_to(weight_row * mis[...], (8, M)).astype(BF16)
    cres8 = jnp.broadcast_to(cres_row, (8, S)).astype(BF16)

    def slot(i, dd, half):
        return (i + dd) % NX, 4 if dd == 2 else 2 * dd + half

    def core_copy(i, dd, half):
        q, n = slot(i, dd, half)
        return copy(
            G2.at[1 - c, q, n], R0.at[q, n],
            core_s.at[dd, half * 4 + i], core_r.at[dd, half * 4 + i], core_dev,
        )

    def gram_half(half):
        def step(i, _):
            at = pl.multiple_of((half * 4 + i) * 128, 128)
            g = dot0(A[:, pl.ds(at, 128)], A[:, pl.ds(at, 640)])
            for d in range(5 - half):
                q, n = slot(i, d // 2, half)
                G2[d % 2, q, n] = g[:, d * 128 : (d + 1) * 128]
            for dd in range(2):
                core_copy(i, dd, half).start()
            if half == 0:

                @pl.when(c == 1)
                def _():
                    core_copy(i, 2, 0).start()

            return 0

        lax.fori_loop(0, 4, step, 0)

    far, right, left = (x + 2) % NX, (x + 1) % NX, (x + 3) % NX

    def x1(n):
        d = 1 if n == 4 else n % 2
        return copy(R0.at[far, n], RX1.at[n], x1_s.at[n], x1_r.at[n], x_dev(1 if d == 0 else 3))

    def x2(d, n):
        return copy(
            R0.at[right if d == 0 else left, n], RX2.at[d, n],
            x2_s.at[d, n], x2_r.at[d, n], x_dev(1 if d == 0 else 3),
        )

    def x_first(n):
        d = 1 if n == 4 else n % 2
        for i in range(4):
            core_copy(i, n // 2, 0 if n == 4 else n % 2).wait_recv()
        R0[:, n] = R0[:, n] + G2[c, :, n]
        x1(n).start()
        x2(1 - d, n).start()

    def x_second(n):
        d = 1 if n == 4 else n % 2
        dest = right if d == 0 else left
        x1(n).wait_recv()
        R0[dest, n] = R0[dest, n] + RX1[n]
        x2(d, n).start()

    def spread(block, strip):
        parts = block.reshape(NY, 2, 8, 128)
        W[0, :, strip] = parts[:, 0]
        W[1, strip] = parts[:, 1]

    def x_last(n):
        for d in range(2):
            x2(d, n).wait_recv()
        own = R0[x, n] + RX2[0, n] + RX2[1, n]
        dd = n // 2
        i = (x + 4 - dd) % NX + (0 if n == 4 else (n % 2) * 4)
        j = (i + 2 * dd + c) % NZ
        if dd == 0:
            spread(own, i)

            @pl.when(c == 1)
            def _():
                spread(own.T, j)

        else:
            spread(own, i)
            spread(own.T, j)

    def only_core0(step, n):
        @pl.when(c == 0)
        def _():
            step(n)

    gram_half(0)
    x_first(0)
    x_first(2)
    gram_half(1)
    only_core0(x_first, 4)
    x_first(1)
    x_first(3)

    GC[0] = (
        jnp.dot(res8, A[:M, :PS], preferred_element_type=F32)
        - jnp.dot(cres8, pm, preferred_element_type=F32)
    )[0:1]
    gc = copy(GC.at[0], GC.at[1], gc_s, gc_r, core_dev)
    gc.start()

    gc.wait_recv()
    GX[x] = GC[0] + GC[1]

    def gx(k):
        return copy(GX.at[x], GX.at[x], gx_s.at[k - 1], gx_r.at[k - 1], x_dev(k))

    for k in range(1, NX):
        gx(k).start()

    state_rows = weight_row * ss[...].astype(F32)
    pair = jnp.concatenate(
        [state_rows * (1.0 - side_f), state_rows * side_f], axis=0
    ).astype(BF16)
    pgram = dot1(pair, pair)
    pcross = jnp.dot(pair, A[:M, :PS], preferred_element_type=F32)
    pgrad = dot1(res8, pair)[0:1]
    HC[...] = pcross[S:] - wide[S:]
    HB[...] = jnp.zeros_like(HB)
    HB[0:S, 0:S] = pgram[S:, S:] + small[S:, S:]
    HB[S : S + 1, 0:S] = pgrad[:, S:] + state_grad[:, S:]
    cross[...] = pcross[:S] + wide[:S]
    hess[...] = pgram[:S, :S] + small[:S, :S]
    ngrad[...] = pgrad[:, :S] - state_grad[:, :S]

    x_second(0)
    x_second(2)
    only_core0(x_second, 4)
    x_second(1)
    x_second(3)

    halo = [
        copy(HC, HCr, h_s.at[0], h_r.at[0], after),
        copy(HB, HBr, h_s.at[1], h_r.at[1], after),
    ]

    @pl.when(seg < NX * NY - 1)
    def _():
        for h in halo:
            h.start()

    for k in range(1, NX):
        gx(k).wait_recv()
    GY[y] = (GX[0] + GX[1]) + (GX[2] + GX[3])

    def gy(k):
        return copy(GY.at[y], GY.at[y], gy_s.at[k - 1], gy_r.at[k - 1], y_dev(k))

    for k in range(1, NY):
        gy(k).start()

    x_last(0)
    x_last(2)
    only_core0(x_last, 4)
    x_last(1)
    x_last(3)

    lines = [(y, y_dev, z, z_dev), (z, z_dev, y, y_dev)]

    def pc(g, k):
        at, dev, _, _ = lines[g]
        return copy(W.at[g, (at + k) % 8], R1.at[g, k - 1], p_s.at[g, k - 1], p_r.at[g, k - 1], dev(k))

    def qc(g, k):
        _, _, at, dev = lines[g]
        return copy(V.at[g, (at + k) % 8], R2.at[g, k - 1], q_s.at[g, k - 1], q_r.at[g, k - 1], dev(k))

    for k in range(1, 8):
        for g in range(2):
            pc(g, k).start()
    for k in range(1, NY):
        gy(k).wait_recv()
    part = GY[0]
    for k in range(1, NY):
        part = part + GY[k]
    GZ[z] = part

    def gz(k):
        return copy(GZ.at[z], GZ.at[z], gz_s.at[k - 1], gz_r.at[k - 1], z_dev(k))

    for k in range(1, NZ):
        gz(k).start()

    @pl.when(seg > 0)
    def _():
        for h in halo:
            h.wait_recv()
        cross[...] = cross[...] + HCr[...]
        hess[...] = hess[...] + HBr[0:S, 0:S]
        ngrad[...] = ngrad[...] + HBr[S : S + 1, 0:S]

    for i in (2, 3, 4):
        results[i].start()

    for g in range(2):
        acc = W[g, lines[g][0]]
        for k in range(1, 8):
            pc(g, k).wait_recv()
            acc = acc + R1[g, k - 1]
        V[g] = acc
        for k in range(1, 8):
            qc(g, k).start()
    for k in range(1, NZ):
        gz(k).wait_recv()
    part = GZ[0]
    for k in range(1, NZ):
        part = part + GZ[k]
    scale = 1.0 / (2 * NX * NY * NZ)
    grad[...] = part * scale
    results[1].start()

    done = []
    for g in range(2):
        own = V[g, lines[g][2]]
        for k in range(1, 8):
            qc(g, k).wait_recv()
            own = own + R2[g, k - 1]
        done.append(own * scale)
    FA[x, y] = done[0]
    FB[y, x] = done[1]

    def ay(g, k):
        block = FA.at[x, y] if g == 0 else FB.at[y]
        return copy(block, block, ay_s.at[g, k - 1], ay_r.at[g, k - 1], y_dev(k))

    def ax(g, k):
        block = FA.at[x] if g == 0 else FB.at[y, x]
        return copy(block, block, ax_s.at[g, k - 1], ax_r.at[g, k - 1], x_dev(k))

    for k in range(1, NY):
        ay(0, k).start()
    for k in range(1, NX):
        ax(1, k).start()
    for k in range(1, NX):
        ax(1, k).wait_recv()
    for k in range(1, NY):
        ay(1, k).start()
    for k in range(1, NY):
        ay(0, k).wait_recv()
    for k in range(1, NX):
        ax(0, k).start()
    for k in range(1, NY):
        ay(1, k).wait_recv()
    for k in range(1, NX):
        ax(0, k).wait_recv()

    mine, theirs = pl.ds(4 * c, 4), pl.ds(4 * (1 - c), 4)
    swap = [
        copy(FA.at[:, theirs], FAr, fin_s.at[0], fin_r.at[0], core_dev),
        copy(FB.at[theirs], FBr, fin_s.at[1], fin_r.at[1], core_dev),
    ]
    for one in swap:
        one.start()

    def place(owner, first, second):
        at = pl.multiple_of(((owner + NZ - z) % NZ) * 128, 128)
        gram[:, pl.ds(at, 128)] = jnp.stack([first, second], axis=1).reshape(64, 128)

    for q in range(NX):
        place(2 * q + c, FA[q, mine], FB[mine, q])
    for one in swap:
        one.wait_recv()
    for q in range(NX):
        place(2 * q + 1 - c, FAr[q], FBr[:, q])
    results[0].start()

    for k in range(1, NX):
        tx(k).wait_send()
        gx(k).wait_send()
        for g in range(2):
            ax(g, k).wait_send()
    for k in range(1, NY):
        ty(k).wait_send()
        gy(k).wait_send()
        for g in range(2):
            ay(g, k).wait_send()
            pc(g, k).wait_send()
            qc(g, k).wait_send()
    for k in range(1, NZ):
        gz(k).wait_send()
    gc.wait_send()

    for one in swap:
        one.wait_send()
    for half in range(2):
        for i in range(4):
            for dd in range(2):
                core_copy(i, dd, half).wait_send()

    def x_drain(n):
        x1(n).wait_send()
        for d in range(2):
            x2(d, n).wait_send()

    for n in range(4):
        x_drain(n)
    only_core0(x_drain, 4)

    @pl.when(c == 1)
    def _():
        for i in range(4):
            core_copy(i, 2, 0).wait_send()

    @pl.when(seg < NX * NY - 1)
    def _():
        for h in halo:
            h.wait_send()

    for out in results:
        out.wait()


def put_out(*refs):
    ins, outs, held, sems = refs[:6], refs[6:12], refs[12:18], refs[18]
    into = [pltpu.make_async_copy(ins[i], held[i], sems.at[0, i]) for i in range(6)]
    back = [pltpu.make_async_copy(held[i], outs[i], sems.at[1, i]) for i in range(6)]
    for one in into:
        one.start()
    for one, two in zip(into, back):
        one.wait()
        two.start()
    for two in back:
        two.wait()


def shards(sp, ss, mis, dep, cc, side, tr, cs, nr, cm):
    vmem = pl.BlockSpec(memory_space=pltpu.VMEM)
    hbm = pl.BlockSpec(memory_space=pltpu.HBM)
    sem = pltpu.SemaphoreType.DMA
    outs = pl.pallas_call(
        kernel,
        out_shape=[jax.ShapeDtypeStruct(s, F32) for s in OUTS],
        in_specs=[vmem if i == 4 else hbm for i in range(10)],
        out_specs=[hbm] * 6,
        scratch_shapes=[pltpu.VMEM(s, F32) for s in OUTS]
        + [
            sem((6,)),
            pltpu.VMEM((M, PS), BF16),
            pltpu.VMEM((S, M), BF16),
            pltpu.VMEM((1, M), F32),
            pltpu.VMEM((1, M), F32),
            pltpu.VMEM((1, M), jnp.int32),
            pltpu.VMEM((S, S), BF16),
            pltpu.VMEM((S, PS), BF16),
            pltpu.VMEM((S, S), F32),
            pltpu.VMEM((1, S), F32),
            sem((9,)),
            pltpu.VMEM((M + S, PS + PS // 2), BF16),
            pltpu.VMEM((2, NX, 5, 128, 128), F32),
            pltpu.VMEM((NX, 5, 128, 128), F32),
            pltpu.VMEM((5, 128, 128), F32),
            pltpu.VMEM((2, 5, 128, 128), F32),
            pltpu.VMEM((2, 8, 8, 8, 128), F32),
            pltpu.VMEM((2, 7, 8, 8, 128), F32),
            pltpu.VMEM((2, 8, 8, 128), F32),
            pltpu.VMEM((2, 7, 8, 128), F32),
            pltpu.VMEM((NX, NY, 8, 128), F32),
            pltpu.VMEM((NY, NX, 8, 128), F32),
            pltpu.VMEM((NX, 4, 8, 128), F32),
            pltpu.VMEM((4, NX, 8, 128), F32),
            pltpu.VMEM((NX, 1, 128), F32),
            pltpu.VMEM((NY, 1, 128), F32),
            pltpu.VMEM((2, 1, PS), F32),
            pltpu.VMEM((NX, 1, PS), F32),
            pltpu.VMEM((NY, 1, PS), F32),
            pltpu.VMEM((NZ, 1, PS), F32),
            pltpu.VMEM((72, 128), F32),
            pltpu.VMEM((S, PS), F32),
            pltpu.VMEM((72, 128), F32),
            pltpu.VMEM((S, PS), F32),
            sem((NX - 1,)), sem((NX - 1,)),
            sem((NY - 1,)), sem((NY - 1,)),
            sem((3, 8)), sem((3, 8)),
            sem((5,)), sem((5,)),
            sem((2, 5)), sem((2, 5)),
            sem((2, 7)), sem((2, 7)),
            sem((2, 7)), sem((2, 7)),
            sem((2,)), sem((2,)),
            sem((2, NY - 1)), sem((2, NY - 1)),
            sem((2, NX - 1)), sem((2, NX - 1)),
            sem, sem,
            sem((NX - 1,)), sem((NX - 1,)),
            sem((NY - 1,)), sem((NY - 1,)),
            sem((NZ - 1,)), sem((NZ - 1,)),
            sem((2,)), sem((2,)),
        ],
        compiler_params=pltpu.CompilerParams(
            collective_id=0, has_side_effects=True, vmem_limit_bytes=VMEM_ALL
        ),
    )(
        sp.reshape(M, PS), ss.reshape(M, S).T, mis.reshape(1, M), dep.reshape(1, M), cc,
        side.reshape(1, M), tr.reshape(S, S), cs.reshape(S, PS), nr.reshape(S, S),
        cm.reshape(1, S),
    )
    outs = pl.pallas_call(
        put_out,
        out_shape=[jax.ShapeDtypeStruct(s, F32) for s in OUTS],
        in_specs=[hbm] * 6,
        out_specs=[hbm] * 6,
        scratch_shapes=[pltpu.VMEM(s, F32) for s in OUTS] + [sem((2, 6))],
        compiler_params=pltpu.CompilerParams(vmem_limit_bytes=VMEM_ALL),
    )(*outs)
    gram, grad, hess, cross, ngrad, coup = outs
    return (
        gram, grad.reshape(PS), hess.reshape(1, 1, S, S), cross.reshape(1, 1, S, PS),
        ngrad.reshape(1, 1, S), coup.reshape(1, 1, S, S),
    )


def solution(mesh):
    wide = P("sat", "seg", None, None)
    line = P("sat", "seg", None)
    return jax.shard_map(
        shards,
        mesh=mesh,
        in_specs=(wide, wide, line, line, P("sat", "seg"), line, wide, wide, wide, line),
        out_specs=(P("sat", None), P(), wide, wide, line, wide),
        check_vma=False,
    )
```

```python
import jax
import jax.numpy as jnp
from jax import lax
from jax.experimental import pallas as pl
from jax.experimental.pallas import tpu as pltpu
from jax.sharding import PartitionSpec as P

highest = lax.Precision.HIGHEST
MESH = pl.DeviceIdType.MESH
F32 = jnp.float32
BF16 = jnp.bfloat16

NX, NY, NZ = 4, 8, 8
M, S, PS = 320, 64, 1024
VMEM_ALL = 67043328
OUTS = [(64, PS), (1, PS), (S, S), (S, PS), (1, S), (S, S)]


def dot0(a, b, precision=None):
    return lax.dot_general(
        a, b, (((0,), (0,)), ((), ())), precision=precision, preferred_element_type=F32
    )


def dot1(a, b):
    return lax.dot_general(a, b, (((1,), (1,)), ((), ())), preferred_element_type=F32)


def kernel(
    sp_h, ss_h, mis_h, dep_h, cc, side_h, tr_h, cs_h, nr_h, cm_h,
    gram_h, grad_h, hess_h, cross_h, ngrad_h, coup_h,
    gram, grad, hess, cross, ngrad, coup, out_s,
    sp, ss, mis, dep, side, tr, cs, nr, cm, in_s,
    A, G2, R0, RX1, RX2, W, R1, V, R2, FA, FB, FAr, FBr,
    TX, TY, GC, GX, GY, GZ, HB, HC, HBr, HCr, HBq, HCq,
    tx_s, tx_r, ty_s, ty_r, core_s, core_r, x1_s, x1_r, x2_s, x2_r,
    p_s, p_r, q_s, q_r, fin_s, fin_r, ay_s, ay_r, ax_s, ax_r,
    gc_s, gc_r, gx_s, gx_r, gy_s, gy_r, gz_s, gz_r, h_s, h_r, q_h_s, q_h_r,
):
    sat = lax.axis_index("sat")
    seg = lax.axis_index("seg")
    z, c = sat // 2, sat % 2
    y, x = seg // NX, seg % NX

    core_dev = (sat + 1 - 2 * c, seg)

    def x_dev(k):
        return (sat, y * NX + (x + k) % NX)

    def y_dev(k):
        return (sat, ((y + k) % NY) * NX + x)

    def z_dev(k):
        return (((z + k) % NZ) * 2 + c, seg)

    def copy(src, dst, send, recv, dev):
        return pltpu.make_async_remote_copy(
            src_ref=src, dst_ref=dst, send_sem=send, recv_sem=recv,
            device_id=dev, device_id_type=MESH,
        )

    loads = [
        pltpu.make_async_copy(a, b, in_s.at[i])
        for i, (a, b) in enumerate(
            [
                (dep_h, dep), (nr_h, nr), (cs_h, cs), (tr_h, tr), (cm_h, cm),
                (mis_h, mis), (side_h, side), (ss_h, ss), (sp_h, sp),
            ]
        )
    ]
    for load in loads:
        load.start()
    results = [
        pltpu.make_async_copy(a, b, out_s.at[i])
        for i, (a, b) in enumerate(
            [
                (gram, gram_h), (grad, grad_h), (hess, hess_h),
                (cross, cross_h), (ngrad, ngrad_h), (coup, coup_h),
            ]
        )
    ]
    barrier = pltpu.get_barrier_semaphore()
    partners = [core_dev]
    partners += [x_dev(k) for k in range(1, NX)]
    partners += [y_dev(k) for k in range(1, NY)]
    partners += [z_dev(k) for k in range(1, NZ)]
    for dev in partners:
        pl.semaphore_signal(barrier, inc=1, device_id=dev, device_id_type=MESH)

    rows = lax.broadcasted_iota(jnp.int32, (M, M), 0)
    lanes = lax.broadcasted_iota(jnp.int32, (M, M), 1)
    count = cc[...]
    loads[0].wait()
    used = jnp.where(lax.broadcasted_iota(jnp.int32, (1, M), 1) < count, dep[...], 0.0)
    through = jnp.sum(used, axis=1, keepdims=True)
    TX[x] = jnp.broadcast_to(through, (1, 128))

    pl.semaphore_wait(barrier, len(partners))

    def tx(k):
        return copy(TX.at[x], TX.at[x], tx_s.at[k - 1], tx_r.at[k - 1], x_dev(k))

    for k in range(1, NX):
        tx(k).start()

    link = jnp.where(seg < NX * NY - 1, 1.0, 0.0).astype(F32)
    r64 = lax.broadcasted_iota(jnp.int32, (S, S), 0)
    l64 = lax.broadcasted_iota(jnp.int32, (S, S), 1)
    for load in loads[1:]:
        load.wait()
    root = (jnp.where(r64 == l64, 1.0, 0.0) + nr[...]) * link
    pm = jnp.dot(
        root, cs[...].astype(F32), precision=highest, preferred_element_type=F32
    ).astype(BF16)
    A[M:, :PS] = pm
    inner = jnp.sum(jnp.where(lanes < rows, used, 0.0), axis=1, keepdims=True)

    for k in range(1, NX):
        tx(k).wait_recv()
    xprior = jnp.zeros((1, 128), F32)
    total = jnp.zeros((1, 128), F32)
    for k in range(NX):
        part = TX[k]
        total = total + part
        xprior = xprior + jnp.where(k < x, part, 0.0)
    TY[y] = total

    def ty(k):
        return copy(TY.at[y], TY.at[y], ty_s.at[k - 1], ty_r.at[k - 1], y_dev(k))

    for k in range(1, NY):
        ty(k).start()

    smap = jnp.dot(
        root, tr[...].astype(F32), precision=highest, preferred_element_type=F32
    )
    both = jnp.concatenate([smap, root], axis=1)
    small = dot0(both, both, highest)
    wide = dot0(both, pm.astype(F32), highest)
    coup[...] = -small[:S, S:]
    results[5].start()
    cres = jnp.sum(root * cm[...], axis=1, keepdims=True).astype(BF16).astype(F32)
    cres_row = jnp.sum(jnp.where(r64 == l64, cres, 0.0), axis=0, keepdims=True)
    state_grad = jnp.sum(both * cres, axis=0, keepdims=True)
    side_f = side[...].astype(F32)
    live_col = jnp.where(
        lax.broadcasted_iota(jnp.int32, (M, 1), 0) < count, 1.0, 0.0
    ).astype(F32)

    for k in range(1, NY):
        ty(k).wait_recv()
    prior = xprior
    for k in range(NY):
        prior = prior + jnp.where(k < y, TY[k], 0.0)

    age = inner + prior[:, 0:1]
    weight = jnp.sqrt(live_col / (1.0 + age * (4.0 / (M * NX * NY))))
    weight_row = jnp.sum(jnp.where(rows == lanes, weight, 0.0), axis=0, keepdims=True)
    A[:M, :PS] = (weight * sp[...].astype(F32)).astype(BF16)
    A[:, PS:] = A[:, : PS // 2]
    res8 = jnp.broadcast_to(weight_row * mis[...], (8, M)).astype(BF16)
    cres8 = jnp.broadcast_to(cres_row, (8, S)).astype(BF16)

    def slot(i, dd, half):
        return (i + dd) % NX, 4 if dd == 2 else 2 * dd + half

    def core_copy(i, dd, half):
        q, n = slot(i, dd, half)
        return copy(
            G2.at[1 - c, q, n], R0.at[q, n],
            core_s.at[dd, half * 4 + i], core_r.at[dd, half * 4 + i], core_dev,
        )

    def gram_half(half):
        def step(i, _):
            at = pl.multiple_of((half * 4 + i) * 128, 128)
            g = dot0(A[:, pl.ds(at, 128)], A[:, pl.ds(at, 640)])
            for d in range(5 - half):
                q, n = slot(i, d // 2, half)
                G2[d % 2, q, n] = g[:, d * 128 : (d + 1) * 128]
            for dd in range(2):
                core_copy(i, dd, half).start()
            if half == 0:

                @pl.when(c == 1)
                def _():
                    core_copy(i, 2, 0).start()

            return 0

        lax.fori_loop(0, 4, step, 0)

    far, right, left = (x + 2) % NX, (x + 1) % NX, (x + 3) % NX

    def x1(n):
        d = 1 if n == 4 else n % 2
        return copy(R0.at[far, n], RX1.at[n], x1_s.at[n], x1_r.at[n], x_dev(1 if d == 0 else 3))

    def x2(d, n):
        return copy(
            R0.at[right if d == 0 else left, n], RX2.at[d, n],
            x2_s.at[d, n], x2_r.at[d, n], x_dev(1 if d == 0 else 3),
        )

    def x_first(n):
        d = 1 if n == 4 else n % 2
        for i in range(4):
            core_copy(i, n // 2, 0 if n == 4 else n % 2).wait_recv()
        R0[:, n] = R0[:, n] + G2[c, :, n]
        x1(n).start()
        x2(1 - d, n).start()

    def x_second(n):
        d = 1 if n == 4 else n % 2
        dest = right if d == 0 else left
        x1(n).wait_recv()
        R0[dest, n] = R0[dest, n] + RX1[n]
        x2(d, n).start()

    def spread(block, strip):
        parts = block.reshape(NY, 2, 8, 128)
        W[0, :, strip] = parts[:, 0]
        W[1, strip] = parts[:, 1]

    def x_last(n):
        for d in range(2):
            x2(d, n).wait_recv()
        own = R0[x, n] + RX2[0, n] + RX2[1, n]
        dd = n // 2
        i = (x + 4 - dd) % NX + (0 if n == 4 else (n % 2) * 4)
        j = (i + 2 * dd + c) % NZ
        if dd == 0:
            spread(own, i)

            @pl.when(c == 1)
            def _():
                spread(own.T, j)

        else:
            spread(own, i)
            spread(own.T, j)

    def only_core0(step, n):
        @pl.when(c == 0)
        def _():
            step(n)

    gram_half(0)
    x_first(0)
    x_first(2)
    gram_half(1)
    only_core0(x_first, 4)
    x_first(1)
    x_first(3)

    GC[0] = (
        jnp.dot(res8, A[:M, :PS], preferred_element_type=F32)
        - jnp.dot(cres8, pm, preferred_element_type=F32)
    )[0:1]
    gc = copy(GC.at[0], GC.at[1], gc_s, gc_r, core_dev)
    gc.start()

    gc.wait_recv()
    GX[x] = GC[0] + GC[1]

    def gx(k):
        return copy(GX.at[x], GX.at[x], gx_s.at[k - 1], gx_r.at[k - 1], x_dev(k))

    for k in range(1, NX):
        gx(k).start()

    state_rows = weight_row * ss[...].astype(F32)
    pair = jnp.concatenate(
        [state_rows * (1.0 - side_f), state_rows * side_f], axis=0
    ).astype(BF16)
    pgram = dot1(pair, pair)
    pcross = jnp.dot(pair, A[:M, :PS], preferred_element_type=F32)
    pgrad = dot1(res8, pair)[0:1]
    HC[...] = pcross[S:] - wide[S:]
    HB[...] = jnp.zeros_like(HB)
    HB[0:S, 0:S] = pgram[S:, S:] + small[S:, S:]
    HB[S : S + 1, 0:S] = pgrad[:, S:] + state_grad[:, S:]
    cross[...] = pcross[:S] + wide[:S]
    hess[...] = pgram[:S, :S] + small[:S, :S]
    ngrad[...] = pgrad[:, :S] - state_grad[:, :S]


    pass_halo = [
        copy(HC, HCq, q_h_s.at[0], q_h_r.at[0], y_dev(1)),
        copy(HB, HBq, q_h_s.at[1], q_h_r.at[1], y_dev(1)),
    ]
    halo = [
        copy(HC, HCr, h_s.at[0], h_r.at[0], x_dev(1)),
        copy(HB, HBr, h_s.at[1], h_r.at[1], x_dev(1)),
    ]
    relay = [
        copy(HCq, HCr, h_s.at[0], h_r.at[0], x_dev(1)),
        copy(HBq, HBr, h_s.at[1], h_r.at[1], x_dev(1)),
    ]
    last_x = x == NX - 1

    @pl.when(last_x & (y < NY - 1))
    def _():
        for h in pass_halo:
            h.start()

    x_second(0)
    x_second(2)
    only_core0(x_second, 4)
    x_second(1)
    x_second(3)

    @pl.when(x < NX - 1)
    def _():
        for h in halo:
            h.start()

    for k in range(1, NX):
        gx(k).wait_recv()
    GY[y] = (GX[0] + GX[1]) + (GX[2] + GX[3])

    def gy(k):
        return copy(GY.at[y], GY.at[y], gy_s.at[k - 1], gy_r.at[k - 1], y_dev(k))

    for k in range(1, NY):
        gy(k).start()

    x_last(0)
    x_last(2)
    only_core0(x_last, 4)
    x_last(1)
    x_last(3)

    lines = [(y, y_dev, z, z_dev), (z, z_dev, y, y_dev)]

    def pc(g, d, j):
        at, dev, _, _ = lines[g]
        to = 1 if d == 0 else -1
        src = W.at[g, (at + to * (j + 1) + 8) % 8]
        dst = R1.at[g, d, j - 1]
        if j == 3:
            src, dst = src.at[pl.ds(4 * d, 4)], dst.at[pl.ds(4 * d, 4)]
        return copy(src, dst, p_s.at[g, d, j - 1], p_r.at[g, d, j - 1], dev((to * j) % 8))

    def pn(g, d):
        at, dev, _, _ = lines[g]
        to = 1 if d == 0 else -1
        return copy(
            W.at[g, (at + to + 8) % 8], R1.at[g, d, 3], p_s.at[g, d, 3], p_r.at[g, d, 3],
            dev(to % 8),
        )

    def qc(g, k):
        _, _, at, dev = lines[g]
        return copy(V.at[g, (at + k) % 8], R2.at[g, k - 1], q_s.at[g, k - 1], q_r.at[g, k - 1], dev(k))

    for j in (3, 2, 1):
        for g in range(2):
            for d in range(2):
                pc(g, d, j).start()
    for g in range(2):
        for d in range(2):
            for j in (1, 2, 3):
                pc(g, d, j).wait_recv()
            at = (lines[g][0] + (1 if d == 0 else 7)) % 8
            lo, hi = 4 * d, 4 * (1 - d)
            W[g, at, pl.ds(lo, 4)] = (
                W[g, at, pl.ds(lo, 4)]
                + R1[g, d, 0, pl.ds(lo, 4)] + R1[g, d, 1, pl.ds(lo, 4)] + R1[g, d, 2, pl.ds(lo, 4)]
            )
            W[g, at, pl.ds(hi, 4)] = (
                W[g, at, pl.ds(hi, 4)] + R1[g, d, 0, pl.ds(hi, 4)] + R1[g, d, 1, pl.ds(hi, 4)]
            )
            pn(g, d).start()
    for k in range(1, NY):
        gy(k).wait_recv()
    part = GY[0]
    for k in range(1, NY):
        part = part + GY[k]
    GZ[z] = part

    def gz(k):
        return copy(GZ.at[z], GZ.at[z], gz_s.at[k - 1], gz_r.at[k - 1], z_dev(k))

    for k in range(1, NZ):
        gz(k).start()

    @pl.when(last_x & (y > 0))
    def _():
        for h, r in zip(pass_halo, relay):
            h.wait_recv()
            r.start()


    for g in range(2):
        for d in range(2):
            pn(g, d).wait_recv()
        V[g] = W[g, lines[g][0]] + R1[g, 0, 3] + R1[g, 1, 3]
        for k in range(1, 8):
            qc(g, k).start()
    for k in range(1, NZ):
        gz(k).wait_recv()
    part = GZ[0]
    for k in range(1, NZ):
        part = part + GZ[k]
    scale = 1.0 / (2 * NX * NY * NZ)
    grad[...] = part * scale
    results[1].start()

    done = []
    for g in range(2):
        own = V[g, lines[g][2]]
        for k in range(1, 8):
            qc(g, k).wait_recv()
            own = own + R2[g, k - 1]
        done.append(own * scale)
    FA[x, y] = done[0]
    FB[y, x] = done[1]

    def ay(g, k):
        block = FA.at[x, y] if g == 0 else FB.at[y]
        return copy(block, block, ay_s.at[g, k - 1], ay_r.at[g, k - 1], y_dev(k))

    def ax(g, k):
        block = FA.at[x] if g == 0 else FB.at[y, x]
        return copy(block, block, ax_s.at[g, k - 1], ax_r.at[g, k - 1], x_dev(k))

    for k in range(1, NY):
        ay(0, k).start()
    for k in range(1, NX):
        ax(1, k).start()
    for k in range(1, NX):
        ax(1, k).wait_recv()
    for k in range(1, NY):
        ay(1, k).start()

    @pl.when(seg > 0)
    def _():
        for h in halo:
            h.wait_recv()
        cross[...] = cross[...] + HCr[...]
        hess[...] = hess[...] + HBr[0:S, 0:S]
        ngrad[...] = ngrad[...] + HBr[S : S + 1, 0:S]

    for i in (2, 3, 4):
        results[i].start()

    for k in range(1, NY):
        ay(0, k).wait_recv()
    for k in range(1, NX):
        ax(0, k).start()
    for k in range(1, NY):
        ay(1, k).wait_recv()
    for k in range(1, NX):
        ax(0, k).wait_recv()

    mine, theirs = pl.ds(4 * c, 4), pl.ds(4 * (1 - c), 4)
    swap = [
        copy(FA.at[:, theirs], FAr, fin_s.at[0], fin_r.at[0], core_dev),
        copy(FB.at[theirs], FBr, fin_s.at[1], fin_r.at[1], core_dev),
    ]
    for one in swap:
        one.start()

    def place(owner, first, second):
        at = pl.multiple_of(((owner + NZ - z) % NZ) * 128, 128)
        gram[:, pl.ds(at, 128)] = jnp.stack([first, second], axis=1).reshape(64, 128)

    for q in range(NX):
        place(2 * q + c, FA[q, mine], FB[mine, q])
    for one in swap:
        one.wait_recv()
    for q in range(NX):
        place(2 * q + 1 - c, FAr[q], FBr[:, q])
    results[0].start()

    for k in range(1, NX):
        tx(k).wait_send()
        gx(k).wait_send()
        for g in range(2):
            ax(g, k).wait_send()
    for k in range(1, NY):
        ty(k).wait_send()
        gy(k).wait_send()
        for g in range(2):
            ay(g, k).wait_send()
            qc(g, k).wait_send()
    for k in range(1, NZ):
        gz(k).wait_send()
    gc.wait_send()

    for one in swap:
        one.wait_send()
    for half in range(2):
        for i in range(4):
            for dd in range(2):
                core_copy(i, dd, half).wait_send()

    def x_drain(n):
        x1(n).wait_send()
        for d in range(2):
            x2(d, n).wait_send()

    for n in range(4):
        x_drain(n)
    only_core0(x_drain, 4)

    @pl.when(c == 1)
    def _():
        for i in range(4):
            core_copy(i, 2, 0).wait_send()

    for g in range(2):
        for d in range(2):
            for j in (1, 2, 3):
                pc(g, d, j).wait_send()
            pn(g, d).wait_send()

    @pl.when(last_x & (y < NY - 1))
    def _():
        for h in pass_halo:
            h.wait_send()

    @pl.when((x < NX - 1) | (y > 0))
    def _():
        for h in halo:
            h.wait_send()

    for out in results:
        out.wait()


def put_out(*refs):
    ins, outs, held, sems = refs[:6], refs[6:12], refs[12:18], refs[18]
    into = [pltpu.make_async_copy(ins[i], held[i], sems.at[0, i]) for i in range(6)]
    back = [pltpu.make_async_copy(held[i], outs[i], sems.at[1, i]) for i in range(6)]
    for one in into:
        one.start()
    for one, two in zip(into, back):
        one.wait()
        two.start()
    for two in back:
        two.wait()


def shards(sp, ss, mis, dep, cc, side, tr, cs, nr, cm):
    vmem = pl.BlockSpec(memory_space=pltpu.VMEM)
    hbm = pl.BlockSpec(memory_space=pltpu.HBM)
    sem = pltpu.SemaphoreType.DMA
    outs = pl.pallas_call(
        kernel,
        out_shape=[jax.ShapeDtypeStruct(s, F32) for s in OUTS],
        in_specs=[vmem if i == 4 else hbm for i in range(10)],
        out_specs=[hbm] * 6,
        scratch_shapes=[pltpu.VMEM(s, F32) for s in OUTS]
        + [
            sem((6,)),
            pltpu.VMEM((M, PS), BF16),
            pltpu.VMEM((S, M), BF16),
            pltpu.VMEM((1, M), F32),
            pltpu.VMEM((1, M), F32),
            pltpu.VMEM((1, M), jnp.int32),
            pltpu.VMEM((S, S), BF16),
            pltpu.VMEM((S, PS), BF16),
            pltpu.VMEM((S, S), F32),
            pltpu.VMEM((1, S), F32),
            sem((9,)),
            pltpu.VMEM((M + S, PS + PS // 2), BF16),
            pltpu.VMEM((2, NX, 5, 128, 128), F32),
            pltpu.VMEM((NX, 5, 128, 128), F32),
            pltpu.VMEM((5, 128, 128), F32),
            pltpu.VMEM((2, 5, 128, 128), F32),
            pltpu.VMEM((2, 8, 8, 8, 128), F32),
            pltpu.VMEM((2, 2, 4, 8, 8, 128), F32),
            pltpu.VMEM((2, 8, 8, 128), F32),
            pltpu.VMEM((2, 7, 8, 128), F32),
            pltpu.VMEM((NX, NY, 8, 128), F32),
            pltpu.VMEM((NY, NX, 8, 128), F32),
            pltpu.VMEM((NX, 4, 8, 128), F32),
            pltpu.VMEM((4, NX, 8, 128), F32),
            pltpu.VMEM((NX, 1, 128), F32),
            pltpu.VMEM((NY, 1, 128), F32),
            pltpu.VMEM((2, 1, PS), F32),
            pltpu.VMEM((NX, 1, PS), F32),
            pltpu.VMEM((NY, 1, PS), F32),
            pltpu.VMEM((NZ, 1, PS), F32),
            pltpu.VMEM((72, 128), F32),
            pltpu.VMEM((S, PS), F32),
            pltpu.VMEM((72, 128), F32),
            pltpu.VMEM((S, PS), F32),
            pltpu.VMEM((72, 128), F32),
            pltpu.VMEM((S, PS), F32),
            sem((NX - 1,)), sem((NX - 1,)),
            sem((NY - 1,)), sem((NY - 1,)),
            sem((3, 8)), sem((3, 8)),
            sem((5,)), sem((5,)),
            sem((2, 5)), sem((2, 5)),
            sem((2, 2, 4)), sem((2, 2, 4)),
            sem((2, 7)), sem((2, 7)),
            sem((2,)), sem((2,)),
            sem((2, NY - 1)), sem((2, NY - 1)),
            sem((2, NX - 1)), sem((2, NX - 1)),
            sem, sem,
            sem((NX - 1,)), sem((NX - 1,)),
            sem((NY - 1,)), sem((NY - 1,)),
            sem((NZ - 1,)), sem((NZ - 1,)),
            sem((2,)), sem((2,)),
            sem((2,)), sem((2,)),
        ],
        compiler_params=pltpu.CompilerParams(
            collective_id=0, has_side_effects=True, vmem_limit_bytes=VMEM_ALL
        ),
    )(
        sp.reshape(M, PS), ss.reshape(M, S).T, mis.reshape(1, M), dep.reshape(1, M), cc,
        side.reshape(1, M), tr.reshape(S, S), cs.reshape(S, PS), nr.reshape(S, S),
        cm.reshape(1, S),
    )
    outs = pl.pallas_call(
        put_out,
        out_shape=[jax.ShapeDtypeStruct(s, F32) for s in OUTS],
        in_specs=[hbm] * 6,
        out_specs=[hbm] * 6,
        scratch_shapes=[pltpu.VMEM(s, F32) for s in OUTS] + [sem((2, 6))],
        compiler_params=pltpu.CompilerParams(vmem_limit_bytes=VMEM_ALL),
    )(*outs)
    gram, grad, hess, cross, ngrad, coup = outs
    return (
        gram, grad.reshape(PS), hess.reshape(1, 1, S, S), cross.reshape(1, 1, S, PS),
        ngrad.reshape(1, 1, S), coup.reshape(1, 1, S, S),
    )


def solution(mesh):
    wide = P("sat", "seg", None, None)
    line = P("sat", "seg", None)
    return jax.shard_map(
        shards,
        mesh=mesh,
        in_specs=(wide, wide, line, line, P("sat", "seg"), line, wide, wide, wide, line),
        out_specs=(P("sat", None), P(), wide, wide, line, wide),
        check_vma=False,
    )
```

```python
import jax
import jax.numpy as jnp
from jax import lax
from jax.experimental import pallas as pl
from jax.experimental.pallas import tpu as pltpu
from jax.sharding import PartitionSpec as P

highest = lax.Precision.HIGHEST
MESH = pl.DeviceIdType.MESH
F32 = jnp.float32
BF16 = jnp.bfloat16

NX, NY, NZ = 4, 8, 8
M, S, PS = 320, 64, 1024
FAR8 = (4, 3, 5, 2, 6, 1, 7)
FAR4 = (2, 1, 3)
VMEM_ALL = 67043328
OUTS = [(64, PS), (1, PS), (S, S), (S, PS), (1, S), (S, S)]


def dot0(a, b, precision=None):
    return lax.dot_general(
        a, b, (((0,), (0,)), ((), ())), precision=precision, preferred_element_type=F32
    )


def dot1(a, b):
    return lax.dot_general(a, b, (((1,), (1,)), ((), ())), preferred_element_type=F32)


def kernel(
    sp_h, ss_h, mis_h, dep_h, cc, side_h, tr_h, cs_h, nr_h, cm_h,
    gram_h, grad_h, hess_h, cross_h, ngrad_h, coup_h,
    gram, grad, hess, cross, ngrad, coup, out_s,
    sp, ss, mis, dep, side, tr, cs, nr, cm, in_s,
    A, G2, R0, RX1, RX2, W, R1, V, R2, FA, FB, FAr, FBr,
    TX, TY, GC, GX, GY, GZ, HB, HC, HBr, HCr, HBq, HCq,
    tx_s, tx_r, ty_s, ty_r, core_s, core_r, x1_s, x1_r, x2_s, x2_r,
    p_s, p_r, q_s, q_r, fin_s, fin_r, ay_s, ay_r, ax_s, ax_r,
    gc_s, gc_r, gx_s, gx_r, gy_s, gy_r, gz_s, gz_r, h_s, h_r, q_h_s, q_h_r,
):
    sat = lax.axis_index("sat")
    seg = lax.axis_index("seg")
    z, c = sat // 2, sat % 2
    y, x = seg // NX, seg % NX

    core_dev = (sat + 1 - 2 * c, seg)

    def x_dev(k):
        return (sat, y * NX + (x + k) % NX)

    def y_dev(k):
        return (sat, ((y + k) % NY) * NX + x)

    def z_dev(k):
        return (((z + k) % NZ) * 2 + c, seg)

    def copy(src, dst, send, recv, dev):
        return pltpu.make_async_remote_copy(
            src_ref=src, dst_ref=dst, send_sem=send, recv_sem=recv,
            device_id=dev, device_id_type=MESH,
        )

    barrier = pltpu.get_barrier_semaphore()
    partners = [dev(k) for k in FAR8 for dev in (y_dev, z_dev)]
    partners += [x_dev(k) for k in FAR4] + [core_dev]
    for dev in partners:
        pl.semaphore_signal(barrier, inc=1, device_id=dev, device_id_type=MESH)

    loads = [
        pltpu.make_async_copy(a, b, in_s.at[i])
        for i, (a, b) in enumerate(
            [
                (dep_h, dep), (nr_h, nr), (cs_h, cs), (tr_h, tr), (cm_h, cm),
                (mis_h, mis), (side_h, side), (ss_h, ss), (sp_h, sp),
            ]
        )
    ]
    for load in loads:
        load.start()
    results = [
        pltpu.make_async_copy(a, b, out_s.at[i])
        for i, (a, b) in enumerate(
            [
                (gram, gram_h), (grad, grad_h), (hess, hess_h),
                (cross, cross_h), (ngrad, ngrad_h), (coup, coup_h),
            ]
        )
    ]

    rows = lax.broadcasted_iota(jnp.int32, (M, M), 0)
    lanes = lax.broadcasted_iota(jnp.int32, (M, M), 1)
    count = cc[...]
    loads[0].wait()
    used = jnp.where(lax.broadcasted_iota(jnp.int32, (1, M), 1) < count, dep[...], 0.0)
    through = jnp.sum(used, axis=1, keepdims=True)
    TX[x] = jnp.broadcast_to(through, (1, 128))

    pl.semaphore_wait(barrier, len(partners))

    def tx(k):
        return copy(TX.at[x], TX.at[x], tx_s.at[k - 1], tx_r.at[k - 1], x_dev(k))

    for k in FAR4:
        tx(k).start()

    link = jnp.where(seg < NX * NY - 1, 1.0, 0.0).astype(F32)
    r64 = lax.broadcasted_iota(jnp.int32, (S, S), 0)
    l64 = lax.broadcasted_iota(jnp.int32, (S, S), 1)
    for load in loads[1:]:
        load.wait()
    root = (jnp.where(r64 == l64, 1.0, 0.0) + nr[...]) * link
    pm = jnp.dot(
        root, cs[...].astype(F32), precision=highest, preferred_element_type=F32
    ).astype(BF16)
    A[M:, :PS] = pm
    inner = jnp.sum(jnp.where(lanes < rows, used, 0.0), axis=1, keepdims=True)

    for k in range(1, NX):
        tx(k).wait_recv()
    xprior = jnp.zeros((1, 128), F32)
    total = jnp.zeros((1, 128), F32)
    for k in range(NX):
        part = TX[k]
        total = total + part
        xprior = xprior + jnp.where(k < x, part, 0.0)
    TY[y] = total

    def ty(k):
        return copy(TY.at[y], TY.at[y], ty_s.at[k - 1], ty_r.at[k - 1], y_dev(k))

    for k in FAR8:
        ty(k).start()

    smap = jnp.dot(
        root, tr[...].astype(F32), precision=highest, preferred_element_type=F32
    )
    both = jnp.concatenate([smap, root], axis=1)
    small = dot0(both, both, highest)
    wide = dot0(both, pm.astype(F32), highest)
    coup[...] = -small[:S, S:]
    results[5].start()
    cres = jnp.sum(root * cm[...], axis=1, keepdims=True).astype(BF16).astype(F32)
    cres_row = jnp.sum(jnp.where(r64 == l64, cres, 0.0), axis=0, keepdims=True)
    state_grad = jnp.sum(both * cres, axis=0, keepdims=True)
    side_f = side[...].astype(F32)
    live_col = jnp.where(
        lax.broadcasted_iota(jnp.int32, (M, 1), 0) < count, 1.0, 0.0
    ).astype(F32)

    for k in range(1, NY):
        ty(k).wait_recv()
    prior = xprior
    for k in range(NY):
        prior = prior + jnp.where(k < y, TY[k], 0.0)

    age = inner + prior[:, 0:1]
    weight = jnp.sqrt(live_col / (1.0 + age * (4.0 / (M * NX * NY))))
    weight_row = jnp.sum(jnp.where(rows == lanes, weight, 0.0), axis=0, keepdims=True)
    A[:M, :PS] = (weight * sp[...].astype(F32)).astype(BF16)
    A[:, PS:] = A[:, : PS // 2]
    res8 = jnp.broadcast_to(weight_row * mis[...], (8, M)).astype(BF16)
    cres8 = jnp.broadcast_to(cres_row, (8, S)).astype(BF16)

    def slot(i, dd, half):
        return (i + dd) % NX, 4 if dd == 2 else 2 * dd + half

    def core_copy(i, dd, half):
        q, n = slot(i, dd, half)
        return copy(
            G2.at[1 - c, q, n], R0.at[q, n],
            core_s.at[dd, half * 4 + i], core_r.at[dd, half * 4 + i], core_dev,
        )

    def gram_half(half):
        def step(i, _):
            at = pl.multiple_of((half * 4 + i) * 128, 128)
            g = dot0(A[:, pl.ds(at, 128)], A[:, pl.ds(at, 640)])
            for d in range(5 - half):
                q, n = slot(i, d // 2, half)
                G2[d % 2, q, n] = g[:, d * 128 : (d + 1) * 128]
            for dd in range(2):
                core_copy(i, dd, half).start()
            if half == 0:

                @pl.when(c == 1)
                def _():
                    core_copy(i, 2, 0).start()

            return 0

        lax.fori_loop(0, 4, step, 0)

    far, right, left = (x + 2) % NX, (x + 1) % NX, (x + 3) % NX

    def x1(n):
        d = 1 if n == 4 else n % 2
        return copy(R0.at[far, n], RX1.at[n], x1_s.at[n], x1_r.at[n], x_dev(1 if d == 0 else 3))

    def x2(d, n):
        return copy(
            R0.at[right if d == 0 else left, n], RX2.at[d, n],
            x2_s.at[d, n], x2_r.at[d, n], x_dev(1 if d == 0 else 3),
        )

    def x_first(n):
        d = 1 if n == 4 else n % 2
        for i in range(4):
            core_copy(i, n // 2, 0 if n == 4 else n % 2).wait_recv()
        R0[:, n] = R0[:, n] + G2[c, :, n]
        x1(n).start()
        x2(1 - d, n).start()

    def x_second(n):
        d = 1 if n == 4 else n % 2
        dest = right if d == 0 else left
        x1(n).wait_recv()
        R0[dest, n] = R0[dest, n] + RX1[n]
        x2(d, n).start()

    def spread(block, strip):
        parts = block.reshape(NY, 2, 8, 128)
        W[0, :, strip] = parts[:, 0]
        W[1, strip] = parts[:, 1]

    def x_last(n):
        for d in range(2):
            x2(d, n).wait_recv()
        own = R0[x, n] + RX2[0, n] + RX2[1, n]
        dd = n // 2
        i = (x + 4 - dd) % NX + (0 if n == 4 else (n % 2) * 4)
        j = (i + 2 * dd + c) % NZ
        if dd == 0:
            spread(own, i)

            @pl.when(c == 1)
            def _():
                spread(own.T, j)

        else:
            spread(own, i)
            spread(own.T, j)

    def only_core0(step, n):
        @pl.when(c == 0)
        def _():
            step(n)

    gram_half(0)
    x_first(0)
    x_first(2)
    gram_half(1)
    only_core0(x_first, 4)
    x_first(1)
    x_first(3)

    GC[0] = (
        jnp.dot(res8, A[:M, :PS], preferred_element_type=F32)
        - jnp.dot(cres8, pm, preferred_element_type=F32)
    )[0:1]
    gc = copy(GC.at[0], GC.at[1], gc_s, gc_r, core_dev)
    gc.start()

    gc.wait_recv()
    GX[x] = GC[0] + GC[1]

    def gx(k):
        return copy(GX.at[x], GX.at[x], gx_s.at[k - 1], gx_r.at[k - 1], x_dev(k))

    for k in FAR4:
        gx(k).start()

    state_rows = weight_row * ss[...].astype(F32)
    pair = jnp.concatenate(
        [state_rows * (1.0 - side_f), state_rows * side_f], axis=0
    ).astype(BF16)
    pgram = dot1(pair, pair)
    pcross = jnp.dot(pair, A[:M, :PS], preferred_element_type=F32)
    pgrad = dot1(res8, pair)[0:1]
    HC[...] = pcross[S:] - wide[S:]
    HB[...] = jnp.zeros_like(HB)
    HB[0:S, 0:S] = pgram[S:, S:] + small[S:, S:]
    HB[S : S + 1, 0:S] = pgrad[:, S:] + state_grad[:, S:]
    cross[...] = pcross[:S] + wide[:S]
    hess[...] = pgram[:S, :S] + small[:S, :S]
    ngrad[...] = pgrad[:, :S] - state_grad[:, :S]


    pass_halo = [
        copy(HC, HCq, q_h_s.at[0], q_h_r.at[0], y_dev(1)),
        copy(HB, HBq, q_h_s.at[1], q_h_r.at[1], y_dev(1)),
    ]
    halo = [
        copy(HC, HCr, h_s.at[0], h_r.at[0], x_dev(1)),
        copy(HB, HBr, h_s.at[1], h_r.at[1], x_dev(1)),
    ]
    relay = [
        copy(HCq, HCr, h_s.at[0], h_r.at[0], x_dev(1)),
        copy(HBq, HBr, h_s.at[1], h_r.at[1], x_dev(1)),
    ]
    last_x = x == NX - 1

    @pl.when(last_x & (y < NY - 1))
    def _():
        for h in pass_halo:
            h.start()

    x_second(0)
    x_second(2)
    only_core0(x_second, 4)
    x_second(1)
    x_second(3)

    @pl.when(x < NX - 1)
    def _():
        for h in halo:
            h.start()

    for k in range(1, NX):
        gx(k).wait_recv()
    GY[y] = (GX[0] + GX[1]) + (GX[2] + GX[3])

    def gy(k):
        return copy(GY.at[y], GY.at[y], gy_s.at[k - 1], gy_r.at[k - 1], y_dev(k))

    for k in FAR8:
        gy(k).start()

    x_last(0)
    x_last(2)
    only_core0(x_last, 4)
    x_last(1)
    x_last(3)

    lines = [(y, y_dev, z, z_dev), (z, z_dev, y, y_dev)]

    def pc(g, d, j):
        at, dev, _, _ = lines[g]
        to = 1 if d == 0 else -1
        src = W.at[g, (at + to * (j + 1) + 8) % 8]
        dst = R1.at[g, d, j - 1]
        if j == 3:
            src, dst = src.at[pl.ds(4 * d, 4)], dst.at[pl.ds(4 * d, 4)]
        return copy(src, dst, p_s.at[g, d, j - 1], p_r.at[g, d, j - 1], dev((to * j) % 8))

    def pn(g, d):
        at, dev, _, _ = lines[g]
        to = 1 if d == 0 else -1
        return copy(
            W.at[g, (at + to + 8) % 8], R1.at[g, d, 3], p_s.at[g, d, 3], p_r.at[g, d, 3],
            dev(to % 8),
        )

    def qc(g, k):
        _, _, at, dev = lines[g]
        return copy(V.at[g, (at + k) % 8], R2.at[g, k - 1], q_s.at[g, k - 1], q_r.at[g, k - 1], dev(k))

    for j in (3, 2, 1):
        for g in range(2):
            for d in range(2):
                pc(g, d, j).start()
    for g in range(2):
        for d in range(2):
            for j in (1, 2, 3):
                pc(g, d, j).wait_recv()
            at = (lines[g][0] + (1 if d == 0 else 7)) % 8
            lo, hi = 4 * d, 4 * (1 - d)
            W[g, at, pl.ds(lo, 4)] = (
                W[g, at, pl.ds(lo, 4)]
                + R1[g, d, 0, pl.ds(lo, 4)] + R1[g, d, 1, pl.ds(lo, 4)] + R1[g, d, 2, pl.ds(lo, 4)]
            )
            W[g, at, pl.ds(hi, 4)] = (
                W[g, at, pl.ds(hi, 4)] + R1[g, d, 0, pl.ds(hi, 4)] + R1[g, d, 1, pl.ds(hi, 4)]
            )
            pn(g, d).start()
    for k in range(1, NY):
        gy(k).wait_recv()
    part = GY[0]
    for k in range(1, NY):
        part = part + GY[k]
    GZ[z] = part

    def gz(k):
        return copy(GZ.at[z], GZ.at[z], gz_s.at[k - 1], gz_r.at[k - 1], z_dev(k))

    for k in FAR8:
        gz(k).start()

    @pl.when(last_x & (y > 0))
    def _():
        for h, r in zip(pass_halo, relay):
            h.wait_recv()
            r.start()


    for g in range(2):
        for d in range(2):
            pn(g, d).wait_recv()
        V[g] = W[g, lines[g][0]] + R1[g, 0, 3] + R1[g, 1, 3]
        for k in FAR8:
            qc(g, k).start()
    for k in range(1, NZ):
        gz(k).wait_recv()
    part = GZ[0]
    for k in range(1, NZ):
        part = part + GZ[k]
    scale = 1.0 / (2 * NX * NY * NZ)
    grad[...] = part * scale
    results[1].start()

    def ay(g, k):
        block = FA.at[x, y] if g == 0 else FB.at[y]
        return copy(block, block, ay_s.at[g, k - 1], ay_r.at[g, k - 1], y_dev(k))

    def ax(g, k):
        block = FA.at[x] if g == 0 else FB.at[y, x]
        return copy(block, block, ax_s.at[g, k - 1], ax_r.at[g, k - 1], x_dev(k))

    for g in range(2):
        own = V[g, lines[g][2]]
        for k in range(1, 8):
            qc(g, k).wait_recv()
            own = own + R2[g, k - 1]
        if g == 0:
            FA[x, y] = own * scale
            for k in FAR8:
                ay(0, k).start()
        else:
            FB[y, x] = own * scale
            for k in FAR4:
                ax(1, k).start()

    for k in range(1, NX):
        ax(1, k).wait_recv()
    for k in FAR8:
        ay(1, k).start()

    for k in range(1, NY):
        ay(0, k).wait_recv()
    for k in FAR4:
        ax(0, k).start()

    @pl.when(seg > 0)
    def _():
        for h in halo:
            h.wait_recv()
        cross[...] = cross[...] + HCr[...]
        hess[...] = hess[...] + HBr[0:S, 0:S]
        ngrad[...] = ngrad[...] + HBr[S : S + 1, 0:S]

    for i in (2, 3, 4):
        results[i].start()

    mine, theirs = pl.ds(4 * c, 4), pl.ds(4 * (1 - c), 4)
    swap = [
        copy(FA.at[:, theirs], FAr, fin_s.at[0], fin_r.at[0], core_dev),
        copy(FB.at[theirs], FBr, fin_s.at[1], fin_r.at[1], core_dev),
    ]
    for k in range(1, NY):
        ay(1, k).wait_recv()
    swap[1].start()
    for k in range(1, NX):
        ax(0, k).wait_recv()

    swap[0].start()

    def place(owner, first, second):
        at = pl.multiple_of(((owner + NZ - z) % NZ) * 128, 128)
        gram[:, pl.ds(at, 128)] = jnp.stack([first, second], axis=1).reshape(64, 128)

    for q in range(NX):
        place(2 * q + c, FA[q, mine], FB[mine, q])
    for one in swap:
        one.wait_recv()
    for q in range(NX):
        place(2 * q + 1 - c, FAr[q], FBr[:, q])
    results[0].start()

    for k in range(1, NX):
        tx(k).wait_send()
        gx(k).wait_send()
        for g in range(2):
            ax(g, k).wait_send()
    for k in range(1, NY):
        ty(k).wait_send()
        gy(k).wait_send()
        for g in range(2):
            ay(g, k).wait_send()
            qc(g, k).wait_send()
    for k in range(1, NZ):
        gz(k).wait_send()
    gc.wait_send()

    for one in swap:
        one.wait_send()
    for half in range(2):
        for i in range(4):
            for dd in range(2):
                core_copy(i, dd, half).wait_send()

    def x_drain(n):
        x1(n).wait_send()
        for d in range(2):
            x2(d, n).wait_send()

    for n in range(4):
        x_drain(n)
    only_core0(x_drain, 4)

    @pl.when(c == 1)
    def _():
        for i in range(4):
            core_copy(i, 2, 0).wait_send()

    for g in range(2):
        for d in range(2):
            for j in (1, 2, 3):
                pc(g, d, j).wait_send()
            pn(g, d).wait_send()

    @pl.when(last_x & (y < NY - 1))
    def _():
        for h in pass_halo:
            h.wait_send()

    @pl.when((x < NX - 1) | (y > 0))
    def _():
        for h in halo:
            h.wait_send()

    for out in results:
        out.wait()


def put_out(*refs):
    ins, outs, held, sems = refs[:6], refs[6:12], refs[12:18], refs[18]
    into = [pltpu.make_async_copy(ins[i], held[i], sems.at[0, i]) for i in range(6)]
    back = [pltpu.make_async_copy(held[i], outs[i], sems.at[1, i]) for i in range(6)]
    for one in into:
        one.start()
    for one, two in zip(into, back):
        one.wait()
        two.start()
    for two in back:
        two.wait()


def shards(sp, ss, mis, dep, cc, side, tr, cs, nr, cm):
    vmem = pl.BlockSpec(memory_space=pltpu.VMEM)
    hbm = pl.BlockSpec(memory_space=pltpu.HBM)
    sem = pltpu.SemaphoreType.DMA
    outs = pl.pallas_call(
        kernel,
        out_shape=[jax.ShapeDtypeStruct(s, F32) for s in OUTS],
        in_specs=[vmem if i == 4 else hbm for i in range(10)],
        out_specs=[hbm] * 6,
        scratch_shapes=[pltpu.VMEM(s, F32) for s in OUTS]
        + [
            sem((6,)),
            pltpu.VMEM((M, PS), BF16),
            pltpu.VMEM((S, M), BF16),
            pltpu.VMEM((1, M), F32),
            pltpu.VMEM((1, M), F32),
            pltpu.VMEM((1, M), jnp.int32),
            pltpu.VMEM((S, S), BF16),
            pltpu.VMEM((S, PS), BF16),
            pltpu.VMEM((S, S), F32),
            pltpu.VMEM((1, S), F32),
            sem((9,)),
            pltpu.VMEM((M + S, PS + PS // 2), BF16),
            pltpu.VMEM((2, NX, 5, 128, 128), F32),
            pltpu.VMEM((NX, 5, 128, 128), F32),
            pltpu.VMEM((5, 128, 128), F32),
            pltpu.VMEM((2, 5, 128, 128), F32),
            pltpu.VMEM((2, 8, 8, 8, 128), F32),
            pltpu.VMEM((2, 2, 4, 8, 8, 128), F32),
            pltpu.VMEM((2, 8, 8, 128), F32),
            pltpu.VMEM((2, 7, 8, 128), F32),
            pltpu.VMEM((NX, NY, 8, 128), F32),
            pltpu.VMEM((NY, NX, 8, 128), F32),
            pltpu.VMEM((NX, 4, 8, 128), F32),
            pltpu.VMEM((4, NX, 8, 128), F32),
            pltpu.VMEM((NX, 1, 128), F32),
            pltpu.VMEM((NY, 1, 128), F32),
            pltpu.VMEM((2, 1, PS), F32),
            pltpu.VMEM((NX, 1, PS), F32),
            pltpu.VMEM((NY, 1, PS), F32),
            pltpu.VMEM((NZ, 1, PS), F32),
            pltpu.VMEM((72, 128), F32),
            pltpu.VMEM((S, PS), F32),
            pltpu.VMEM((72, 128), F32),
            pltpu.VMEM((S, PS), F32),
            pltpu.VMEM((72, 128), F32),
            pltpu.VMEM((S, PS), F32),
            sem((NX - 1,)), sem((NX - 1,)),
            sem((NY - 1,)), sem((NY - 1,)),
            sem((3, 8)), sem((3, 8)),
            sem((5,)), sem((5,)),
            sem((2, 5)), sem((2, 5)),
            sem((2, 2, 4)), sem((2, 2, 4)),
            sem((2, 7)), sem((2, 7)),
            sem((2,)), sem((2,)),
            sem((2, NY - 1)), sem((2, NY - 1)),
            sem((2, NX - 1)), sem((2, NX - 1)),
            sem, sem,
            sem((NX - 1,)), sem((NX - 1,)),
            sem((NY - 1,)), sem((NY - 1,)),
            sem((NZ - 1,)), sem((NZ - 1,)),
            sem((2,)), sem((2,)),
            sem((2,)), sem((2,)),
        ],
        compiler_params=pltpu.CompilerParams(
            collective_id=0, has_side_effects=True, vmem_limit_bytes=VMEM_ALL
        ),
    )(
        sp.reshape(M, PS), ss.reshape(M, S).T, mis.reshape(1, M), dep.reshape(1, M), cc,
        side.reshape(1, M), tr.reshape(S, S), cs.reshape(S, PS), nr.reshape(S, S),
        cm.reshape(1, S),
    )
    outs = pl.pallas_call(
        put_out,
        out_shape=[jax.ShapeDtypeStruct(s, F32) for s in OUTS],
        in_specs=[hbm] * 6,
        out_specs=[hbm] * 6,
        scratch_shapes=[pltpu.VMEM(s, F32) for s in OUTS] + [sem((2, 6))],
        compiler_params=pltpu.CompilerParams(vmem_limit_bytes=VMEM_ALL),
    )(*outs)
    gram, grad, hess, cross, ngrad, coup = outs
    return (
        gram, grad.reshape(PS), hess.reshape(1, 1, S, S), cross.reshape(1, 1, S, PS),
        ngrad.reshape(1, 1, S), coup.reshape(1, 1, S, S),
    )


def solution(mesh):
    wide = P("sat", "seg", None, None)
    line = P("sat", "seg", None)
    return jax.shard_map(
        shards,
        mesh=mesh,
        in_specs=(wide, wide, line, line, P("sat", "seg"), line, wide, wide, wide, line),
        out_specs=(P("sat", None), P(), wide, wide, line, wide),
        check_vma=False,
    )
```

```python
import jax
import jax.numpy as jnp
from jax import lax
from jax.experimental import pallas as pl
from jax.experimental.pallas import tpu as pltpu
from jax.sharding import PartitionSpec as P

highest = lax.Precision.HIGHEST
MESH = pl.DeviceIdType.MESH
F32 = jnp.float32
BF16 = jnp.bfloat16

NX, NY, NZ = 4, 8, 8
M, S, PS = 320, 64, 1024
FAR8 = (4, 3, 5, 2, 6, 1, 7)
FAR4 = (2, 1, 3)
VMEM_ALL = 67043328
OUTS = [(64, PS), (1, PS), (S, S), (S, PS), (1, S), (S, S)]


def dot0(a, b, precision=None):
    return lax.dot_general(
        a, b, (((0,), (0,)), ((), ())), precision=precision, preferred_element_type=F32
    )


def dot1(a, b):
    return lax.dot_general(a, b, (((1,), (1,)), ((), ())), preferred_element_type=F32)


def kernel(
    sp_h, ss_h, mis_h, dep_h, cc, side_h, tr_h, cs_h, nr_h, cm_h,
    gram_h, grad_h, hess_h, cross_h, ngrad_h, coup_h,
    gram, grad, hess, cross, ngrad, coup, out_s,
    sp, ss, mis, dep, side, tr, cs, nr, cm, in_s,
    A, G2, R0, RX1, RX2, W, R1, V, R2, FA, FB, FAr, FBr,
    TX, TY, GC, GX, GY, GZ, HB, HC, HBr, HCr, HBq, HCq,
    tx_s, tx_r, ty_s, ty_r, core_s, core_r, x1_s, x1_r, x2_s, x2_r,
    p_s, p_r, q_s, q_r, fin_s, fin_r, ay_s, ay_r, ax_s, ax_r,
    gc_s, gc_r, gx_s, gx_r, gy_s, gy_r, gz_s, gz_r, h_s, h_r, q_h_s, q_h_r,
):
    sat = lax.axis_index("sat")
    seg = lax.axis_index("seg")
    z, c = sat // 2, sat % 2
    y, x = seg // NX, seg % NX

    core_dev = (sat + 1 - 2 * c, seg)

    def x_dev(k):
        return (sat, y * NX + (x + k) % NX)

    def y_dev(k):
        return (sat, ((y + k) % NY) * NX + x)

    def z_dev(k):
        return (((z + k) % NZ) * 2 + c, seg)

    def copy(src, dst, send, recv, dev):
        return pltpu.make_async_remote_copy(
            src_ref=src, dst_ref=dst, send_sem=send, recv_sem=recv,
            device_id=dev, device_id_type=MESH,
        )

    barrier = pltpu.get_barrier_semaphore()
    partners = [dev(k) for k in FAR8 for dev in (y_dev, z_dev)]
    partners += [x_dev(k) for k in FAR4] + [core_dev]
    for dev in partners:
        pl.semaphore_signal(barrier, inc=1, device_id=dev, device_id_type=MESH)

    loads = [
        pltpu.make_async_copy(a, b, in_s.at[i])
        for i, (a, b) in enumerate(
            [
                (dep_h, dep), (nr_h, nr), (cs_h, cs), (tr_h, tr), (cm_h, cm),
                (mis_h, mis), (side_h, side), (ss_h, ss), (sp_h, sp),
            ]
        )
    ]
    for load in loads:
        load.start()
    results = [
        pltpu.make_async_copy(a, b, out_s.at[i])
        for i, (a, b) in enumerate(
            [
                (gram, gram_h), (grad, grad_h), (hess, hess_h),
                (cross, cross_h), (ngrad, ngrad_h), (coup, coup_h),
            ]
        )
    ]

    rows = lax.broadcasted_iota(jnp.int32, (M, M), 0)
    lanes = lax.broadcasted_iota(jnp.int32, (M, M), 1)
    count = cc[...]
    loads[0].wait()
    used = jnp.where(lax.broadcasted_iota(jnp.int32, (1, M), 1) < count, dep[...], 0.0)
    through = jnp.sum(used, axis=1, keepdims=True)
    TX[x] = jnp.broadcast_to(through, (1, 128))

    pl.semaphore_wait(barrier, len(partners))

    def tx(k):
        return copy(TX.at[x], TX.at[x], tx_s.at[k - 1], tx_r.at[k - 1], x_dev(k))

    for k in FAR4:
        tx(k).start()

    link = jnp.where(seg < NX * NY - 1, 1.0, 0.0).astype(F32)
    r64 = lax.broadcasted_iota(jnp.int32, (S, S), 0)
    l64 = lax.broadcasted_iota(jnp.int32, (S, S), 1)
    for load in loads[1:]:
        load.wait()
    root = (jnp.where(r64 == l64, 1.0, 0.0) + nr[...]) * link
    pm = jnp.dot(
        root, cs[...].astype(F32), precision=highest, preferred_element_type=F32
    ).astype(BF16)
    A[M:, :PS] = pm
    inner = jnp.sum(jnp.where(lanes < rows, used, 0.0), axis=1, keepdims=True)

    for k in range(1, NX):
        tx(k).wait_recv()
    xprior = jnp.zeros((1, 128), F32)
    total = jnp.zeros((1, 128), F32)
    for k in range(NX):
        part = TX[k]
        total = total + part
        xprior = xprior + jnp.where(k < x, part, 0.0)
    TY[y] = total

    def ty(k):
        return copy(TY.at[y], TY.at[y], ty_s.at[k - 1], ty_r.at[k - 1], y_dev(k))

    for k in FAR8:
        ty(k).start()

    smap = jnp.dot(
        root, tr[...].astype(F32), precision=highest, preferred_element_type=F32
    )
    both = jnp.concatenate([smap, root], axis=1)
    small = dot0(both, both, highest)
    wide = dot0(both, pm.astype(F32), highest)
    coup[...] = -small[:S, S:]
    results[5].start()
    cres = jnp.sum(root * cm[...], axis=1, keepdims=True).astype(BF16).astype(F32)
    cres_row = jnp.sum(jnp.where(r64 == l64, cres, 0.0), axis=0, keepdims=True)
    state_grad = jnp.sum(both * cres, axis=0, keepdims=True)
    side_f = side[...].astype(F32)
    live_col = jnp.where(
        lax.broadcasted_iota(jnp.int32, (M, 1), 0) < count, 1.0, 0.0
    ).astype(F32)

    for k in range(1, NY):
        ty(k).wait_recv()
    prior = xprior
    for k in range(NY):
        prior = prior + jnp.where(k < y, TY[k], 0.0)

    age = inner + prior[:, 0:1]
    weight = jnp.sqrt(live_col / (1.0 + age * (4.0 / (M * NX * NY))))
    weight_row = jnp.sum(jnp.where(rows == lanes, weight, 0.0), axis=0, keepdims=True)
    A[:M, :PS] = (weight * sp[...].astype(F32)).astype(BF16)
    A[:, PS:] = A[:, : PS // 2]
    res8 = jnp.broadcast_to(weight_row * mis[...], (8, M)).astype(BF16)
    cres8 = jnp.broadcast_to(cres_row, (8, S)).astype(BF16)

    def slot(i, dd, half):
        return (i + dd) % NX, 4 if dd == 2 else 2 * dd + half

    def core_copy(i, dd, half):
        q, n = slot(i, dd, half)
        return copy(
            G2.at[1 - c, q, n], R0.at[q, n],
            core_s.at[dd, half * 4 + i], core_r.at[dd, half * 4 + i], core_dev,
        )

    def gram_half(half):
        def step(i, _):
            at = pl.multiple_of((half * 4 + i) * 128, 128)
            g = dot0(A[:, pl.ds(at, 128)], A[:, pl.ds(at, 640)])
            for d in range(5 - half):
                q, n = slot(i, d // 2, half)
                G2[d % 2, q, n] = g[:, d * 128 : (d + 1) * 128]
            for dd in range(2):
                core_copy(i, dd, half).start()
            if half == 0:

                @pl.when(c == 1)
                def _():
                    core_copy(i, 2, 0).start()

            return 0

        lax.fori_loop(0, 4, step, 0)

    far, right, left = (x + 2) % NX, (x + 1) % NX, (x + 3) % NX

    def x1(n):
        d = 1 if n == 4 else n % 2
        return copy(R0.at[far, n], RX1.at[n], x1_s.at[n], x1_r.at[n], x_dev(1 if d == 0 else 3))

    def x2(d, n):
        return copy(
            R0.at[right if d == 0 else left, n], RX2.at[d, n],
            x2_s.at[d, n], x2_r.at[d, n], x_dev(1 if d == 0 else 3),
        )

    def x_first(n):
        d = 1 if n == 4 else n % 2
        for i in range(4):
            core_copy(i, n // 2, 0 if n == 4 else n % 2).wait_recv()
        R0[:, n] = R0[:, n] + G2[c, :, n]
        x1(n).start()
        x2(1 - d, n).start()

    def x_second(n):
        d = 1 if n == 4 else n % 2
        dest = right if d == 0 else left
        x1(n).wait_recv()
        R0[dest, n] = R0[dest, n] + RX1[n]
        x2(d, n).start()

    def spread(block, strip):
        parts = block.reshape(NY, 2, 8, 128)
        W[0, :, strip] = parts[:, 0]
        W[1, strip] = parts[:, 1]

    def x_last(n):
        for d in range(2):
            x2(d, n).wait_recv()
        own = R0[x, n] + RX2[0, n] + RX2[1, n]
        dd = n // 2
        i = (x + 4 - dd) % NX + (0 if n == 4 else (n % 2) * 4)
        j = (i + 2 * dd + c) % NZ
        if dd == 0:
            spread(own, i)

            @pl.when(c == 1)
            def _():
                spread(own.T, j)

        else:
            spread(own, i)
            spread(own.T, j)

    def only_core0(step, n):
        @pl.when(c == 0)
        def _():
            step(n)

    gram_half(0)
    x_first(0)
    x_first(2)
    gram_half(1)
    only_core0(x_first, 4)
    x_first(1)
    x_first(3)

    GC[0] = (
        jnp.dot(res8, A[:M, :PS], preferred_element_type=F32)
        - jnp.dot(cres8, pm, preferred_element_type=F32)
    )[0:1]
    gc = copy(GC.at[0], GC.at[1], gc_s, gc_r, core_dev)
    gc.start()

    gc.wait_recv()
    GX[x] = GC[0] + GC[1]

    def gx(k):
        return copy(GX.at[x], GX.at[x], gx_s.at[k - 1], gx_r.at[k - 1], x_dev(k))

    for k in FAR4:
        gx(k).start()

    state_rows = weight_row * ss[...].astype(F32)
    pair = jnp.concatenate(
        [state_rows * (1.0 - side_f), state_rows * side_f], axis=0
    ).astype(BF16)
    pgram = dot1(pair, pair)
    pcross = jnp.dot(pair, A[:M, :PS], preferred_element_type=F32)
    pgrad = dot1(res8, pair)[0:1]
    HC[...] = pcross[S:] - wide[S:]
    HB[...] = jnp.zeros_like(HB)
    HB[0:S, 0:S] = pgram[S:, S:] + small[S:, S:]
    HB[S : S + 1, 0:S] = pgrad[:, S:] + state_grad[:, S:]


    pass_halo = [
        copy(HC, HCq, q_h_s.at[0], q_h_r.at[0], y_dev(1)),
        copy(HB, HBq, q_h_s.at[1], q_h_r.at[1], y_dev(1)),
    ]
    halo = [
        copy(HC, HCr, h_s.at[0], h_r.at[0], x_dev(1)),
        copy(HB, HBr, h_s.at[1], h_r.at[1], x_dev(1)),
    ]
    relay = [
        copy(HCq, HCr, h_s.at[0], h_r.at[0], x_dev(1)),
        copy(HBq, HBr, h_s.at[1], h_r.at[1], x_dev(1)),
    ]
    last_x = x == NX - 1

    @pl.when(last_x & (y < NY - 1))
    def _():
        for h in pass_halo:
            h.start()

    x_second(0)
    x_second(2)
    only_core0(x_second, 4)
    x_second(1)
    x_second(3)

    @pl.when(x < NX - 1)
    def _():
        for h in halo:
            h.start()

    cross[...] = pcross[:S] + wide[:S]
    hess[...] = pgram[:S, :S] + small[:S, :S]
    ngrad[...] = pgrad[:, :S] - state_grad[:, :S]

    for k in range(1, NX):
        gx(k).wait_recv()
    GY[y] = (GX[0] + GX[1]) + (GX[2] + GX[3])

    def gy(k):
        return copy(GY.at[y], GY.at[y], gy_s.at[k - 1], gy_r.at[k - 1], y_dev(k))

    for k in FAR8:
        gy(k).start()

    x_last(0)
    x_last(2)
    only_core0(x_last, 4)
    x_last(1)
    x_last(3)

    lines = [(y, y_dev, z, z_dev), (z, z_dev, y, y_dev)]

    def pc(g, d, j):
        at, dev, _, _ = lines[g]
        to = 1 if d == 0 else -1
        src = W.at[g, (at + to * (j + 1) + 8) % 8]
        dst = R1.at[g, d, j - 1]
        if j == 3:
            src, dst = src.at[pl.ds(4 * d, 4)], dst.at[pl.ds(4 * d, 4)]
        return copy(src, dst, p_s.at[g, d, j - 1], p_r.at[g, d, j - 1], dev((to * j) % 8))

    def pn(g, d):
        at, dev, _, _ = lines[g]
        to = 1 if d == 0 else -1
        return copy(
            W.at[g, (at + to + 8) % 8], R1.at[g, d, 3], p_s.at[g, d, 3], p_r.at[g, d, 3],
            dev(to % 8),
        )

    def qc(g, k):
        _, _, at, dev = lines[g]
        return copy(V.at[g, (at + k) % 8], R2.at[g, k - 1], q_s.at[g, k - 1], q_r.at[g, k - 1], dev(k))

    for j in (3, 2, 1):
        for g in range(2):
            for d in range(2):
                pc(g, d, j).start()
    for g in range(2):
        for d in range(2):
            for j in (1, 2, 3):
                pc(g, d, j).wait_recv()
            at = (lines[g][0] + (1 if d == 0 else 7)) % 8
            lo, hi = 4 * d, 4 * (1 - d)
            W[g, at, pl.ds(lo, 4)] = (
                W[g, at, pl.ds(lo, 4)]
                + R1[g, d, 0, pl.ds(lo, 4)] + R1[g, d, 1, pl.ds(lo, 4)] + R1[g, d, 2, pl.ds(lo, 4)]
            )
            W[g, at, pl.ds(hi, 4)] = (
                W[g, at, pl.ds(hi, 4)] + R1[g, d, 0, pl.ds(hi, 4)] + R1[g, d, 1, pl.ds(hi, 4)]
            )
            pn(g, d).start()
    for k in range(1, NY):
        gy(k).wait_recv()
    part = GY[0]
    for k in range(1, NY):
        part = part + GY[k]
    GZ[z] = part

    def gz(k):
        return copy(GZ.at[z], GZ.at[z], gz_s.at[k - 1], gz_r.at[k - 1], z_dev(k))

    for k in FAR8:
        gz(k).start()

    @pl.when(last_x & (y > 0))
    def _():
        for h, r in zip(pass_halo, relay):
            h.wait_recv()
            r.start()


    for g in range(2):
        for d in range(2):
            pn(g, d).wait_recv()
        V[g] = W[g, lines[g][0]] + R1[g, 0, 3] + R1[g, 1, 3]
        for k in FAR8:
            qc(g, k).start()
    for k in range(1, NZ):
        gz(k).wait_recv()
    part = GZ[0]
    for k in range(1, NZ):
        part = part + GZ[k]
    scale = 1.0 / (2 * NX * NY * NZ)
    grad[...] = part * scale
    results[1].start()

    def ay(g, k):
        block = FA.at[x, y] if g == 0 else FB.at[y]
        return copy(block, block, ay_s.at[g, k - 1], ay_r.at[g, k - 1], y_dev(k))

    def ax(g, k):
        block = FA.at[x] if g == 0 else FB.at[y, x]
        return copy(block, block, ax_s.at[g, k - 1], ax_r.at[g, k - 1], x_dev(k))

    for g in range(2):
        own = V[g, lines[g][2]]
        for k in range(1, 8):
            qc(g, k).wait_recv()
            own = own + R2[g, k - 1]
        if g == 0:
            FA[x, y] = own * scale
            for k in FAR8:
                ay(0, k).start()
        else:
            FB[y, x] = own * scale
            for k in FAR4:
                ax(1, k).start()

    for k in range(1, NX):
        ax(1, k).wait_recv()
    for k in FAR8:
        ay(1, k).start()

    for k in range(1, NY):
        ay(0, k).wait_recv()
    for k in FAR4:
        ax(0, k).start()

    @pl.when(seg > 0)
    def _():
        for h in halo:
            h.wait_recv()
        cross[...] = cross[...] + HCr[...]
        hess[...] = hess[...] + HBr[0:S, 0:S]
        ngrad[...] = ngrad[...] + HBr[S : S + 1, 0:S]

    for i in (2, 3, 4):
        results[i].start()

    mine, theirs = pl.ds(4 * c, 4), pl.ds(4 * (1 - c), 4)
    swap = [
        copy(FA.at[:, theirs], FAr, fin_s.at[0], fin_r.at[0], core_dev),
        copy(FB.at[theirs], FBr, fin_s.at[1], fin_r.at[1], core_dev),
    ]
    for k in range(1, NY):
        ay(1, k).wait_recv()
    swap[1].start()
    for k in range(1, NX):
        ax(0, k).wait_recv()

    swap[0].start()

    def place(owner, first, second):
        at = pl.multiple_of(((owner + NZ - z) % NZ) * 128, 128)
        gram[:, pl.ds(at, 128)] = jnp.stack([first, second], axis=1).reshape(64, 128)

    for q in range(NX):
        place(2 * q + c, FA[q, mine], FB[mine, q])
    for one in swap:
        one.wait_recv()
    for q in range(NX):
        place(2 * q + 1 - c, FAr[q], FBr[:, q])
    results[0].start()

    for k in range(1, NX):
        tx(k).wait_send()
        gx(k).wait_send()
        for g in range(2):
            ax(g, k).wait_send()
    for k in range(1, NY):
        ty(k).wait_send()
        gy(k).wait_send()
        for g in range(2):
            ay(g, k).wait_send()
            qc(g, k).wait_send()
    for k in range(1, NZ):
        gz(k).wait_send()
    gc.wait_send()

    for one in swap:
        one.wait_send()
    for half in range(2):
        for i in range(4):
            for dd in range(2):
                core_copy(i, dd, half).wait_send()

    def x_drain(n):
        x1(n).wait_send()
        for d in range(2):
            x2(d, n).wait_send()

    for n in range(4):
        x_drain(n)
    only_core0(x_drain, 4)

    @pl.when(c == 1)
    def _():
        for i in range(4):
            core_copy(i, 2, 0).wait_send()

    for g in range(2):
        for d in range(2):
            for j in (1, 2, 3):
                pc(g, d, j).wait_send()
            pn(g, d).wait_send()

    @pl.when(last_x & (y < NY - 1))
    def _():
        for h in pass_halo:
            h.wait_send()

    @pl.when((x < NX - 1) | (y > 0))
    def _():
        for h in halo:
            h.wait_send()

    for out in results:
        out.wait()


def put_out(*refs):
    ins, outs, held, sems = refs[:6], refs[6:12], refs[12:18], refs[18]
    into = [pltpu.make_async_copy(ins[i], held[i], sems.at[0, i]) for i in range(6)]
    back = [pltpu.make_async_copy(held[i], outs[i], sems.at[1, i]) for i in range(6)]
    for one in into:
        one.start()
    for one, two in zip(into, back):
        one.wait()
        two.start()
    for two in back:
        two.wait()


def shards(sp, ss, mis, dep, cc, side, tr, cs, nr, cm):
    vmem = pl.BlockSpec(memory_space=pltpu.VMEM)
    hbm = pl.BlockSpec(memory_space=pltpu.HBM)
    sem = pltpu.SemaphoreType.DMA
    outs = pl.pallas_call(
        kernel,
        out_shape=[jax.ShapeDtypeStruct(s, F32) for s in OUTS],
        in_specs=[vmem if i == 4 else hbm for i in range(10)],
        out_specs=[hbm] * 6,
        scratch_shapes=[pltpu.VMEM(s, F32) for s in OUTS]
        + [
            sem((6,)),
            pltpu.VMEM((M, PS), BF16),
            pltpu.VMEM((S, M), BF16),
            pltpu.VMEM((1, M), F32),
            pltpu.VMEM((1, M), F32),
            pltpu.VMEM((1, M), jnp.int32),
            pltpu.VMEM((S, S), BF16),
            pltpu.VMEM((S, PS), BF16),
            pltpu.VMEM((S, S), F32),
            pltpu.VMEM((1, S), F32),
            sem((9,)),
            pltpu.VMEM((M + S, PS + PS // 2), BF16),
            pltpu.VMEM((2, NX, 5, 128, 128), F32),
            pltpu.VMEM((NX, 5, 128, 128), F32),
            pltpu.VMEM((5, 128, 128), F32),
            pltpu.VMEM((2, 5, 128, 128), F32),
            pltpu.VMEM((2, 8, 8, 8, 128), F32),
            pltpu.VMEM((2, 2, 4, 8, 8, 128), F32),
            pltpu.VMEM((2, 8, 8, 128), F32),
            pltpu.VMEM((2, 7, 8, 128), F32),
            pltpu.VMEM((NX, NY, 8, 128), F32),
            pltpu.VMEM((NY, NX, 8, 128), F32),
            pltpu.VMEM((NX, 4, 8, 128), F32),
            pltpu.VMEM((4, NX, 8, 128), F32),
            pltpu.VMEM((NX, 1, 128), F32),
            pltpu.VMEM((NY, 1, 128), F32),
            pltpu.VMEM((2, 1, PS), F32),
            pltpu.VMEM((NX, 1, PS), F32),
            pltpu.VMEM((NY, 1, PS), F32),
            pltpu.VMEM((NZ, 1, PS), F32),
            pltpu.VMEM((72, 128), F32),
            pltpu.VMEM((S, PS), F32),
            pltpu.VMEM((72, 128), F32),
            pltpu.VMEM((S, PS), F32),
            pltpu.VMEM((72, 128), F32),
            pltpu.VMEM((S, PS), F32),
            sem((NX - 1,)), sem((NX - 1,)),
            sem((NY - 1,)), sem((NY - 1,)),
            sem((3, 8)), sem((3, 8)),
            sem((5,)), sem((5,)),
            sem((2, 5)), sem((2, 5)),
            sem((2, 2, 4)), sem((2, 2, 4)),
            sem((2, 7)), sem((2, 7)),
            sem((2,)), sem((2,)),
            sem((2, NY - 1)), sem((2, NY - 1)),
            sem((2, NX - 1)), sem((2, NX - 1)),
            sem, sem,
            sem((NX - 1,)), sem((NX - 1,)),
            sem((NY - 1,)), sem((NY - 1,)),
            sem((NZ - 1,)), sem((NZ - 1,)),
            sem((2,)), sem((2,)),
            sem((2,)), sem((2,)),
        ],
        compiler_params=pltpu.CompilerParams(
            collective_id=0, has_side_effects=True, vmem_limit_bytes=VMEM_ALL
        ),
    )(
        sp.reshape(M, PS), ss.reshape(M, S).T, mis.reshape(1, M), dep.reshape(1, M), cc,
        side.reshape(1, M), tr.reshape(S, S), cs.reshape(S, PS), nr.reshape(S, S),
        cm.reshape(1, S),
    )
    outs = pl.pallas_call(
        put_out,
        out_shape=[jax.ShapeDtypeStruct(s, F32) for s in OUTS],
        in_specs=[hbm] * 6,
        out_specs=[hbm] * 6,
        scratch_shapes=[pltpu.VMEM(s, F32) for s in OUTS] + [sem((2, 6))],
        compiler_params=pltpu.CompilerParams(vmem_limit_bytes=VMEM_ALL),
    )(*outs)
    gram, grad, hess, cross, ngrad, coup = outs
    return (
        gram, grad.reshape(PS), hess.reshape(1, 1, S, S), cross.reshape(1, 1, S, PS),
        ngrad.reshape(1, 1, S), coup.reshape(1, 1, S, S),
    )


def solution(mesh):
    wide = P("sat", "seg", None, None)
    line = P("sat", "seg", None)
    return jax.shard_map(
        shards,
        mesh=mesh,
        in_specs=(wide, wide, line, line, P("sat", "seg"), line, wide, wide, wide, line),
        out_specs=(P("sat", None), P(), wide, wide, line, wide),
        check_vma=False,
    )
```
